32 devices in a mesh: dp: 16 (over z, x, core), tensor: 2 (over y).
Axes of the slice: x: 2, y: 2, z: 4, core: 2. Of those that a mesh axis runs over, the one named last changes fastest.
Arguments:
- tokens: bfloat16 [8192, 2048], P('dp'), may hold values from -6 to 6
- segments: int32 [16, 512], P('dp'), may hold values from 0 to 3, never falling along the last dimension, each value on 1 to 384 neighbouring positions
- cotangent: bfloat16 [8192, 2048], P('dp'), may hold values from -6 to 6
- norm_gain: float32 [2048], P('dp'), may hold values from 0.1 to 1.9
- attn_weight: float32 [2048, 4, 2048], P('dp', None, 'tensor'), may hold values from -0.125 to 0.125
- beta_weight: float32 [2048, 16], P('dp', 'tensor'), may hold values from -0.125 to 0.125
- conv_weight: float32 [3, 4, 16, 128], P(None, None, 'tensor', 'dp'), may hold values from -3 to 3
- out_gain: float32 [128], P('dp'), may hold values from 0.1 to 1.9
- mlp_gain: float32 [2048], P('dp'), may hold values from 0.1 to 1.9
- mlp_weight: float32 [2048, 3, 5632], P('dp', None, 'tensor'), may hold values from -0.125 to 0.125
Outputs:
- output: bfloat16 [8192, 2048], P('dp')
- input_grad: float32 [8192, 2048], P('dp')
- norm_gain_grad: float32 [2048], P('dp')
- attn_weight_grad: float32 [2048, 4, 2048], P('dp', None, 'tensor')
- beta_weight_grad: float32 [2048, 16], P('dp', 'tensor')
- conv_weight_grad: float32 [3, 4, 16, 128], P(None, None, 'tensor', 'dp')
- out_gain_grad: float32 [128], P('dp')
- mlp_gain_grad: float32 [2048], P('dp')
- mlp_weight_grad: float32 [2048, 3, 5632], P('dp', None, 'tensor')
The draws below stay inside these ranges and needn't reach their ends.
Inputs may be any that keep to these rules, and one draw needn't show every extreme that they name: `segments`: within a sequence the numbers never fall; a document (a run of one number) has 1 to 384 tokens, and some document has exactly 384.
All inputs are finite; a program needn't handle non-finite values.
Results may differ from the reference program's by a relative error of at most 0.017.
The reference program's roundings to bfloat16 on the way count: a program that leaves them out, or rounds other values in their place, can miss the bound.
Values may be sent and summed in bfloat16 or wider, within the bound.
No kernel may reach another device: no remote copies, remote signals or barrier semaphores. Data moves between devices by JAX's collectives and lax.ppermute only.
A program may use at most 384 MiB of HBM per device.

```python
import math
import jax
import jax.numpy as jnp
import numpy as np
from jax import lax

D = 2048
HEADS = 16
HEAD_DIM = 128
FF = 5632
BLOCK = 64
LEN = 512
SEQS = 16
TOKENS = 8192
DOCS = 4
DOC_MOST = 384


def levels(key, extent, cuts, smallest, largest):
    gain, own = 1.0, jax.random.fold_in(key, 6)
    for dim, parts in cuts:
        heights = jnp.exp(jax.random.uniform(jax.random.fold_in(own, dim), (parts,), jnp.float32, smallest / len(cuts), largest / len(cuts)))
        gain = gain * jnp.repeat(heights, extent[dim] // parts).reshape([-1 if axis == dim else 1 for axis in range(len(extent))])
    return gain


def length_profile(amount, total, limit, skew):
    weights = [(1 << 20) // math.isqrt(rank ** skew) + 1 for rank in range(2, amount + 1)]
    spare, holding = total - limit - (amount - 1), [1] * (amount - 1)
    while spare > 0:
        candidates = [i for i in range(amount - 1) if holding[i] < limit]
        mass, remaining = sum([weights[i] for i in candidates]), spare
        for i in candidates:
            extra = min(limit - holding[i], max(1, remaining * weights[i] // mass), spare)
            holding[i] = holding[i] + extra
            spare = spare - extra
    return np.array([limit] + holding)


def uneven_parts(stream_key, count, total, most, skew):
    if count == 2:
        one = jax.random.randint(stream_key, (), max(1, total - most), min(most, total - 1) + 1)
        return jnp.stack([one, total - one])
    tallies = jnp.asarray(length_profile(count, total, most, skew), jnp.int32)
    couples = (count - 1) // 2
    source_of, receiver = tallies[1:1 + 2 * couples:2], tallies[2:2 + 2 * couples:2]
    room = jnp.minimum(source_of - 1, most - receiver)
    moved = jax.random.randint(jax.random.fold_in(stream_key, 1), (couples,), 0, 1 << 20) % (room + 1)
    tallies = tallies.at[1:1 + 2 * couples:2].set(source_of - moved).at[2:2 + 2 * couples:2].set(receiver + moved)
    return tallies[jax.random.permutation(jax.random.fold_in(stream_key, 2), count)]


def bell_draw(stream_key, extent, width, limit, cuts=(), held_as=jnp.bfloat16):
    values = jax.random.normal(stream_key, extent, jnp.float32) * width
    if len(cuts) > 0:
        values = levels(stream_key, extent, cuts, -0.22, 0.18) * values
    return jnp.clip(values, min=-limit, max=limit).astype(held_as)


def setup_inputs(seed: int = 0) -> dict:
    arg_keys = jax.random.split(jax.random.key(seed), 11)
    return {
        "tokens": bell_draw(arg_keys[0], (TOKENS, D), 1.0, 6.0, ((0, 16),)),
        "segments": jax.vmap(lambda own: jnp.searchsorted(jnp.cumsum(uneven_parts(own, DOCS, LEN, DOC_MOST, 2)), jnp.arange(LEN), side="right"))(jax.random.split(arg_keys[1], SEQS)).reshape((SEQS, LEN)).astype(jnp.int32),
        "cotangent": bell_draw(arg_keys[2], (TOKENS, D), 1.0, 6.0, ((0, 16),)),
        "norm_gain": jnp.clip(1.0 + 0.18 * jax.random.normal(arg_keys[3], (D,), jnp.float32), 0.1, 1.9),
        "attn_weight": bell_draw(arg_keys[4], (D, 4, D), D ** -0.5, 0.125, ((0, 16), (2, 2)), jnp.float32),
        "beta_weight": bell_draw(arg_keys[5], (D, HEADS), D ** -0.5, 0.125, ((0, 16), (1, 2)), jnp.float32),
        "conv_weight": bell_draw(arg_keys[6], (3, 4, HEADS, HEAD_DIM), 0.5, 3.0, ((2, 2), (3, 16)), jnp.float32),
        "out_gain": jnp.clip(1.0 + 0.18 * jax.random.normal(arg_keys[7], (HEAD_DIM,), jnp.float32), 0.1, 1.9),
        "mlp_gain": jnp.clip(1.0 + 0.18 * jax.random.normal(arg_keys[8], (D,), jnp.float32), 0.1, 1.9),
        "mlp_weight": bell_draw(arg_keys[9], (D, 3, FF), D ** -0.5, 0.125, ((0, 16), (2, 2)), jnp.float32),
    }


highest = lax.Precision.HIGHEST

@jax.custom_vjp
def low(v):
    return lax.optimization_barrier(v.astype(jnp.bfloat16)).astype(jnp.float32)

@jax.custom_vjp
def low_back(v):
    return v

def low_keep(v):
    return (low(v), None)

def low_pass(kept, grad):
    return (grad,)

def back_keep(v):
    return (v, None)

def back_low(kept, grad):
    return (low(grad),)
low.defvjp(low_keep, low_pass)
low_back.defvjp(back_keep, back_low)

def rms_scale(values, gain_values, epsilon):
    return values * lax.rsqrt(lax.optimization_barrier(jnp.mean(values * values, axis=-1, keepdims=True)) + epsilon) * gain_values

def short_conv(signal, weight, seg_ids):
    length = signal.shape[0]
    summed = signal * weight[3]
    for offset in range(1, 4):
        pad_rows = jnp.zeros((offset,) + signal.shape[1:], signal.dtype)
        shifted = jnp.concatenate([pad_rows, signal[:length - offset]], axis=0)
        prior_ids = jnp.concatenate([jnp.full((offset,), -1, jnp.int32), seg_ids[:length - offset]], axis=0)
        allowed = (prior_ids == seg_ids).astype(signal.dtype)
        summed = summed + shifted * allowed[:, None, None] * weight[3 - offset]
    return summed

def delta_block(memory, inputs):
    queries, key_vecs, values, strength, seg_ids, prior_id = inputs
    block_len = seg_ids.shape[0]
    carry_in = (seg_ids == prior_id).astype(queries.dtype)
    same_doc = (seg_ids[:, None] == seg_ids[None, :]).astype(queries.dtype)
    row_ids = jnp.arange(block_len)
    strict = (row_ids[:, None] > row_ids[None, :]).astype(queries.dtype)
    causal = (row_ids[:, None] >= row_ids[None, :]).astype(queries.dtype)
    key_inner = jnp.einsum('ihd,jhd->hij', key_vecs, key_vecs, precision=highest) * (same_doc * strict)
    weights_t = jnp.transpose(strength)
    system = jnp.eye(block_len, dtype=queries.dtype) + weights_t[:, :, None] * key_inner
    recalled = jnp.einsum('hvd,ihd->hiv', memory, key_vecs, precision=highest)
    target = weights_t[:, :, None] * (jnp.transpose(values, (1, 0, 2)) - carry_in[None, :, None] * recalled)
    writes = lax.linalg.triangular_solve(system, target, left_side=True, lower=True, unit_diagonal=True)
    scores = jnp.einsum('ihd,jhd->hij', queries, key_vecs, precision=highest) * (same_doc * causal)
    carried = jnp.einsum('hvd,ihd->hiv', memory, queries, precision=highest)
    output = carry_in[None, :, None] * carried + jnp.einsum('hij,hjv->hiv', scores, writes, precision=highest)
    final_doc = same_doc[block_len - 1]
    updated = carry_in[block_len - 1] * memory + jnp.einsum('hjv,jhd->hvd', writes * final_doc[None, :, None], key_vecs, precision=highest)
    return (updated, jnp.transpose(output, (1, 0, 2)))

def delta_sequence(queries, key_vecs, values, strength, seg_ids):
    length = queries.shape[0]
    head_count = queries.shape[1]
    head_width = queries.shape[2]
    block_count = length // BLOCK
    prior_ids = jnp.concatenate([jnp.full((1,), -1, jnp.int32), seg_ids[BLOCK - 1:length - 1:BLOCK]], axis=0)

    def blocked(array_in):
        return array_in.reshape((block_count, BLOCK) + array_in.shape[1:])
    initial = jnp.zeros((head_count, head_width, head_width), queries.dtype)
    final_state, outputs = lax.scan(jax.checkpoint(delta_block), initial, (blocked(queries), blocked(key_vecs), blocked(values), blocked(strength), blocked(seg_ids), prior_ids))
    return outputs.reshape(queries.shape)

def token_mixer(projected, beta_logits, conv_weight, out_gain, seg_ids):
    length = projected.shape[0]
    convolved = [jax.nn.silu(short_conv(projected[:, which], conv_weight[which], seg_ids)) for which in range(3)]
    queries = convolved[0] * lax.rsqrt(lax.optimization_barrier(jnp.sum(convolved[0] * convolved[0], axis=-1, keepdims=True)) + 1e-06)
    key_vecs = convolved[1] * lax.rsqrt(lax.optimization_barrier(jnp.sum(convolved[1] * convolved[1], axis=-1, keepdims=True)) + 1e-06)
    strength = jax.nn.sigmoid(beta_logits)
    output = delta_sequence(queries, key_vecs, convolved[2], strength, seg_ids)
    return rms_scale(output, out_gain, 1e-05).reshape(length, -1)

def layer_forward(token_in, seg_group, norm_gain, attn_weight, beta_weight, conv_weight, out_gain, mlp_gain, mlp_weight):
    norm_gain = low(norm_gain)
    attn_weight = low(attn_weight)
    beta_weight = low(beta_weight)
    conv_weight = low(conv_weight)
    out_gain = low(out_gain)
    mlp_gain = low(mlp_gain)
    mlp_weight = low(mlp_weight)
    row_count = token_in.shape[0]
    group_seqs = seg_group.shape[0]
    normed = low(rms_scale(token_in, norm_gain, 1e-05))
    projected = low_back(jnp.dot(normed, attn_weight[:, :3].reshape(D, 3 * D), precision=highest))
    beta_logits = low_back(jnp.dot(normed, beta_weight, precision=highest))
    mixed = jax.vmap(token_mixer, in_axes=(0, 0, None, None, 0))(projected.reshape(group_seqs, LEN, 3, HEADS, HEAD_DIM), beta_logits.reshape(group_seqs, LEN, HEADS), conv_weight, out_gain, seg_group)
    mixed = low(mixed.reshape(row_count, D))
    attended = low_back(jnp.dot(mixed, attn_weight[:, 3].T, precision=highest))
    hidden = token_in + attended
    normed_mlp = low(rms_scale(hidden, mlp_gain, 1e-05))
    gate_up = low_back(jnp.dot(normed_mlp, mlp_weight[:, :2].reshape(D, 2 * FF), precision=highest)).reshape(row_count, 2, FF)
    activated = low(jax.nn.silu(gate_up[:, 0]) * gate_up[:, 1])
    down_part = low_back(jnp.dot(activated, mlp_weight[:, 2].T, precision=highest))
    return hidden + down_part

def reference(tokens, segments, cotangent, norm_gain, attn_weight, beta_weight, conv_weight, out_gain, mlp_gain, mlp_weight):
    grouped = max(1, min(SEQS, 4096 // LEN))
    grouped = grouped if SEQS % grouped == 0 else 1
    group_count = SEQS // grouped
    weights = (norm_gain, attn_weight, beta_weight, conv_weight, out_gain, mlp_gain, mlp_weight)
    token_groups = tokens.astype(jnp.float32).reshape(group_count, grouped * LEN, D)
    grad_groups = cotangent.astype(jnp.float32).reshape(group_count, grouped * LEN, D)
    seg_groups = segments.reshape(group_count, grouped, LEN)

    def accumulate(summed, batch_item):
        token_part, grad_part, seg_part = batch_item

        def forward(token_value, *params):
            return layer_forward(token_value, seg_part, *params)
        result, pullback = jax.vjp(forward, token_part, *weights)
        gradients = pullback(grad_part)
        summed = tuple((running + fresh for running, fresh in zip(summed, gradients[1:])))
        return (summed, (result.astype(jnp.bfloat16), gradients[0]))
    initial = tuple((jnp.zeros_like(weight) for weight in weights))
    summed, (results, input_grads) = lax.scan(accumulate, initial, (token_groups, grad_groups, seg_groups))
    return (results.reshape(TOKENS, D), input_grads.reshape(TOKENS, D), summed[0], summed[1], summed[2], summed[3], summed[4], summed[5], summed[6])
```

```python
import functools

import jax
import jax.numpy as jnp
from jax import lax
from jax.experimental import pallas as pl
from jax.experimental.pallas import tpu as pltpu
from jax.sharding import PartitionSpec as P

F32 = jnp.float32
BF16 = jnp.bfloat16
CHUNK = 128
NN = (((1,), (0,)), ((), ()))
NT = (((1,), (1,)), ((), ()))
TN = (((0,), (0,)), ((), ()))


def split2(value):
    high = value.astype(BF16)
    return high, (value - high.astype(F32)).astype(BF16)


def dot1(left, right, dims):
    return lax.dot_general(left, right, dims, preferred_element_type=F32)


def mul3(left, right, dims):
    (lh, ll), (rh, rl) = left, right
    return dot1(lh, rh, dims) + (dot1(lh, rl, dims) + dot1(ll, rh, dims))


def mul1(left, right, dims):
    return dot1(left[0], right[0], dims)


def iotas(size):
    return (
        lax.broadcasted_iota(jnp.int32, (size, size), 0),
        lax.broadcasted_iota(jnp.int32, (size, size), 1),
    )


def allowed_rows(seg_full, offset):
    rows = lax.broadcasted_iota(jnp.int32, seg_full.shape, 0)
    earlier = pltpu.roll(seg_full, offset, 0)
    return jnp.where((earlier == seg_full) & (rows >= offset), 1.0, 0.0).astype(F32)


def conv_taps(signal, taps, gates):
    summed = signal * taps[3:4]
    for offset in range(1, 4):
        summed = summed + pltpu.roll(signal, offset, 0) * gates[offset - 1] * taps[3 - offset : 4 - offset]
    return summed


def chunk_masks(segc_ref, segr_ref, chunk):
    start = chunk * CHUNK
    col = segc_ref[start : start + CHUNK, :]
    row = segr_ref[:, start : start + CHUNK]
    same = col == row
    last = segc_ref[start + CHUNK - 1 : start + CHUNK, :]
    if chunk == 0:
        carry = jnp.zeros(col.shape, F32)
        carry_last = jnp.zeros(last.shape, F32)
    else:
        prior = segc_ref[start - 1 : start, :]
        carry = (col == prior).astype(F32)
        carry_last = (last == prior).astype(F32)
    tail = (col == last).astype(F32)
    return same, carry, carry_last, tail


def head_logits(beta_ref, head):
    lanes = lax.broadcasted_iota(jnp.int32, beta_ref.shape, 1)
    return jnp.sum(jnp.where(lanes == head, beta_ref[...], 0.0), axis=1, keepdims=True)


def forward_kernel(heads, passes, proj_ref, beta_ref, conv_ref, gain_ref, segc_ref, segr_ref,
                   mixed_ref, out_ref, writes_ref, solve_ref, state_ref, q_scr, k_scr, v_scr):
    group = pl.program_id(0)
    length = proj_ref.shape[0]
    chunks = length // CHUNK
    width = 128
    mul = mul3 if passes == 3 else mul1
    seg_full = jnp.broadcast_to(segc_ref[...], (length, width))
    gates = [allowed_rows(seg_full, offset) for offset in (1, 2, 3)]
    betas = []
    for h in range(heads):
        for which, scr in enumerate((q_scr, k_scr, v_scr)):
            column = (which * heads + h) * width
            signal = proj_ref[:, column : column + width]
            mixed_in = conv_taps(signal, conv_ref[which, :, h * width : (h + 1) * width], gates)
            value = mixed_in * jax.nn.sigmoid(mixed_in)
            if which < 2:
                value = value * lax.rsqrt(jnp.sum(value * value, axis=1, keepdims=True) + 1e-6)
            scr[:, h * width : (h + 1) * width] = value
        betas.append(jax.nn.sigmoid(head_logits(beta_ref, group * heads + h)))
    rows, cols = iotas(CHUNK)
    masks = [chunk_masks(segc_ref, segr_ref, c) for c in range(chunks)]
    items = [(h, c) for c in range(chunks) for h in range(heads)]

    def part(scr, h, c):
        return scr[c * CHUNK : (c + 1) * CHUNK, h * width : (h + 1) * width]

    def beta_of(h, c):
        return betas[h][c * CHUNK : (c + 1) * CHUNK]

    system, inverse = {}, {}
    for h, c in items:
        keys = split2(part(k_scr, h, c))
        inner = mul(keys, keys, NT)
        keep = masks[c][0] & (rows > cols)
        system[h, c] = jnp.where(keep, inner * beta_of(h, c), 0.0)
        first = (rows // 2 == cols // 2)
        inverse[h, c] = jnp.where(rows == cols, 1.0, jnp.where(first, -system[h, c], 0.0))
    size = 2
    while size < CHUNK:
        off = (rows // (2 * size) == cols // (2 * size)) & (rows // size != cols // size)
        mid = {}
        for it in items:
            step = jnp.where(off, system[it], 0.0)
            if passes == 3:
                mid[it] = mul3(split2(inverse[it]), split2(step), NN)
            else:
                mid[it] = dot1(inverse[it].astype(BF16), step.astype(BF16), NN)
        for it in items:
            if passes == 3:
                inverse[it] = inverse[it] - mul3(split2(mid[it]), split2(inverse[it]), NN)
            else:
                inverse[it] = inverse[it] - dot1(mid[it].astype(BF16), inverse[it].astype(BF16), NN)
        size *= 2
    scores, fresh, decay = {}, {}, {}
    for h, c in items:
        same, carry, carry_last, tail = masks[c]
        keys, queries, values = part(k_scr, h, c), part(q_scr, h, c), part(v_scr, h, c)
        scores[h, c] = split2(jnp.where(same & (rows >= cols), mul(split2(queries), split2(keys), NT), 0.0))
        solver = split2(inverse[h, c])
        fresh[h, c] = mul(solver, split2(values * beta_of(h, c)), NN)
        decay[h, c] = split2(mul(solver, split2(keys * (beta_of(h, c) * carry)), NN))
        solve_ref[c * CHUNK : (c + 1) * CHUNK, h * width : (h + 1) * width] = inverse[h, c]
    state = {h: jnp.zeros((width, width), F32) for h in range(heads)}
    gain = gain_ref[...]
    for c in range(chunks):
        same, carry, carry_last, tail = masks[c]
        span = slice(c * CHUNK, (c + 1) * CHUNK)
        for h in range(heads):
            state_ref[span, h * width : (h + 1) * width] = state[h]
        writes = {}
        if c == 0:
            for h in range(heads):
                writes[h] = fresh[h, c]
        else:
            split_state = {h: split2(state[h]) for h in range(heads)}
            for h in range(heads):
                writes[h] = fresh[h, c] - mul(decay[h, c], split_state[h], NN)
        for h in range(heads):
            lanes = slice(h * width, (h + 1) * width)
            writes_ref[span, lanes] = writes[h]
            result = mul(scores[h, c], split2(writes[h]), NN)
            if c > 0:
                result = result + carry * mul(split2(part(q_scr, h, c)), split_state[h], NN)
            out_ref[span, lanes] = result
            scale = lax.rsqrt(jnp.mean(result * result, axis=1, keepdims=True) + 1e-5)
            mixed_ref[span, lanes] = (result * scale * gain).astype(BF16)
        if c + 1 < chunks:
            for h in range(heads):
                add = mul(split2(part(k_scr, h, c)), split2(writes[h] * tail), TN)
                state[h] = carry_last * state[h] + add


def backward_kernel(heads, passes, proj_ref, beta_ref, conv_ref, gain_ref, segc_ref, segr_ref,
                    out_ref, writes_ref, solve_ref, state_ref, gmix_ref,
                    gproj_ref, gbeta_ref, gconv_ref, ggain_ref,
                    q_scr, k_scr, v_scr, gq_scr, gk_scr, gv_scr, do_scr):
    group = pl.program_id(0)
    length = proj_ref.shape[0]
    chunks = length // CHUNK
    width = 128
    mul = mul3 if passes == 3 else mul1
    seg_full = jnp.broadcast_to(segc_ref[...], (length, width))
    gates = [allowed_rows(seg_full, offset) for offset in (1, 2, 3)]
    gain = gain_ref[...]

    @pl.when(group == 0)
    def _():
        gbeta_ref[...] = jnp.zeros_like(gbeta_ref)
        ggain_ref[...] = jnp.zeros_like(ggain_ref)

    def convolved(which, h):
        column = (which * heads + h) * width
        signal = proj_ref[:, column : column + width]
        mixed_in = conv_taps(signal, conv_ref[which, :, h * width : (h + 1) * width], gates)
        gate = jax.nn.sigmoid(mixed_in)
        return signal, mixed_in, gate

    betas = []
    for h in range(heads):
        lanes = slice(h * width, (h + 1) * width)
        for which, scr in enumerate((q_scr, k_scr, v_scr)):
            _, mixed_in, gate = convolved(which, h)
            value = mixed_in * gate
            if which < 2:
                value = value * lax.rsqrt(jnp.sum(value * value, axis=1, keepdims=True) + 1e-6)
            scr[:, lanes] = value
        betas.append(jax.nn.sigmoid(head_logits(beta_ref, group * heads + h)))
        result, grad = out_ref[:, lanes], gmix_ref[:, lanes]
        scale = lax.rsqrt(jnp.mean(result * result, axis=1, keepdims=True) + 1e-5)
        unit = result * scale
        ggain_ref[...] += jnp.sum(unit * grad, axis=0, keepdims=True)
        scaled = grad * gain
        do_scr[:, lanes] = scale * (scaled - unit * jnp.mean(unit * scaled, axis=1, keepdims=True))
    rows, cols = iotas(CHUNK)
    masks = [chunk_masks(segc_ref, segr_ref, c) for c in range(chunks)]
    items = [(h, c) for c in range(chunks) for h in range(heads)]

    def part(scr, h, c):
        return scr[c * CHUNK : (c + 1) * CHUNK, h * width : (h + 1) * width]

    def beta_of(h, c):
        return betas[h][c * CHUNK : (c + 1) * CHUNK]

    inner, base, reach, gscore = {}, {}, {}, {}
    for h, c in items:
        same, carry, carry_last, tail = masks[c]
        keys, queries = split2(part(k_scr, h, c)), split2(part(q_scr, h, c))
        grads, writes = split2(part(do_scr, h, c)), split2(part(writes_ref, h, c))
        inner[h, c] = mul(keys, keys, NT)
        causal = same & (rows >= cols)
        scores = split2(jnp.where(causal, mul(queries, keys, NT), 0.0))
        solver = split2(part(solve_ref, h, c))
        base[h, c] = mul(solver, split2(mul(scores, grads, TN)), TN)
        if c + 1 < chunks:
            reach[h, c] = split2(mul(solver, split2(part(k_scr, h, c) * tail), TN))
        gscore = split2(jnp.where(causal, mul(grads, writes, NT), 0.0))
        gq = mul(gscore, keys, NN)
        gk = mul(gscore, queries, TN)
        span, lanes = slice(c * CHUNK, (c + 1) * CHUNK), slice(h * width, (h + 1) * width)
        if c > 0:
            gq = gq + mul(split2(part(do_scr, h, c) * carry), split2(part(state_ref, h, c)), NT)
        gq_scr[span, lanes] = gq
        gk_scr[span, lanes] = gk
    gstate = {}
    gbetas = {}
    for c in reversed(range(chunks)):
        same, carry, carry_last, tail = masks[c]
        span = slice(c * CHUNK, (c + 1) * CHUNK)
        gtarget = {}
        for h in range(heads):
            gtarget[h] = base[h, c]
            if c + 1 < chunks:
                gtarget[h] = gtarget[h] + mul(reach[h, c], split2(gstate[h]), NN)
        for h in range(heads):
            lanes = slice(h * width, (h + 1) * width)
            gk = gk_scr[span, lanes]
            keys = split2(part(k_scr, h, c))
            beta = beta_of(h, c)
            writes = part(writes_ref, h, c)
            split_target = split2(gtarget[h])
            if c + 1 < chunks:
                gk = gk + mul(split2(writes * tail), split2(gstate[h]), NT)
            strict = same & (rows > cols)
            gsys = jnp.where(strict, mul(split_target, split2(writes), NT), 0.0)
            ginner = split2(gsys * beta)
            gbeta = -jnp.sum(gsys * inner[h, c], axis=1, keepdims=True)
            gk = gk - mul(ginner, keys, NN) - mul(ginner, keys, TN)
            target = part(v_scr, h, c)
            if c > 0:
                states = split2(part(state_ref, h, c))
                target = target - carry * mul(keys, states, NN)
                grecall = gtarget[h] * (beta * carry)
                split_recall = split2(grecall)
                gk = gk - mul(split_recall, states, NT)
                new_state = mul(split2(part(q_scr, h, c)), split2(part(do_scr, h, c) * carry), TN)
                new_state = new_state - mul(keys, split_recall, TN)
                if c + 1 < chunks:
                    new_state = new_state + carry_last * gstate[h]
                gstate[h] = new_state
            gbeta = gbeta + jnp.sum(gtarget[h] * target, axis=1, keepdims=True)
            gbetas[h, c] = gbeta * beta * (1.0 - beta)
            gk_scr[span, lanes] = gk
            gv_scr[span, lanes] = gtarget[h] * beta
    for c in range(chunks):
        span = slice(c * CHUNK, (c + 1) * CHUNK)
        lane_ids = lax.broadcasted_iota(jnp.int32, (CHUNK, gbeta_ref.shape[1]), 1)
        total = gbeta_ref[span, :]
        for h in range(heads):
            total = jnp.where(lane_ids == group * heads + h, gbetas[h, c], total)
        gbeta_ref[span, :] = total
    for h in range(heads):
        lanes = slice(h * width, (h + 1) * width)
        for which, (scr, gscr) in enumerate(((q_scr, gq_scr), (k_scr, gk_scr), (v_scr, gv_scr))):
            signal, mixed_in, gate = convolved(which, h)
            grad = gscr[:, lanes]
            if which < 2:
                value = mixed_in * gate
                scale = lax.rsqrt(jnp.sum(value * value, axis=1, keepdims=True) + 1e-6)
                unit = value * scale
                grad = scale * (grad - unit * jnp.sum(unit * grad, axis=1, keepdims=True))
            grad = grad * gate * (1.0 + mixed_in * (1.0 - gate))
            taps = conv_ref[which, :, h * width : (h + 1) * width]
            gsignal = grad * taps[3:4]
            gtaps = [None] * 4
            gtaps[3] = jnp.sum(grad * signal, axis=0, keepdims=True)
            for offset in range(1, 4):
                gated = grad * gates[offset - 1]
                gtaps[3 - offset] = jnp.sum(gated * pltpu.roll(signal, offset, 0), axis=0, keepdims=True)
                gsignal = gsignal + pltpu.roll(gated, length - offset, 0) * taps[3 - offset : 4 - offset]
            gconv_ref[which, :, lanes] = jnp.concatenate(gtaps, axis=0)
            column = (which * heads + h) * width
            gproj_ref[:, column : column + width] = gsignal.astype(BF16)


def mixer_forward(projected, logits, conv, gain, seg_ids, heads, passes):
    length, columns = projected.shape
    groups = columns // (3 * heads * 128)
    wide = heads * 128
    f32 = lambda: jax.ShapeDtypeStruct((length, groups * wide), F32)
    block = pl.BlockSpec((length, wide), lambda g: (0, g))
    fixed = lambda shape: pl.BlockSpec(shape, lambda g: (0,) * len(shape))
    return pl.pallas_call(
        functools.partial(forward_kernel, heads, passes),
        grid=(groups,),
        in_specs=[
            pl.BlockSpec((length, 3 * wide), lambda g: (0, g)),
            fixed((length, 128)),
            pl.BlockSpec((3, 4, wide), lambda g: (0, 0, g)),
            fixed((1, 128)),
            fixed((length, 1)),
            fixed((1, length)),
        ],
        out_specs=[block] * 5,
        out_shape=[jax.ShapeDtypeStruct((length, groups * wide), BF16), f32(), f32(), f32(), f32()],
        scratch_shapes=[pltpu.VMEM((length, wide), F32)] * 3,
        compiler_params=pltpu.CompilerParams(vmem_limit_bytes=56 * 2**20),
        name="mixer_forward",
    )(projected, logits, conv, gain, seg_ids[:, None], seg_ids[None, :])


def mixer_backward(projected, logits, conv, gain, seg_ids, saved, grad_mixed, heads, passes):
    length, columns = projected.shape
    groups = columns // (3 * heads * 128)
    wide = heads * 128
    block = pl.BlockSpec((length, wide), lambda g: (0, g))
    fixed = lambda shape: pl.BlockSpec(shape, lambda g: (0,) * len(shape))
    triple = pl.BlockSpec((length, 3 * wide), lambda g: (0, g))
    taps = pl.BlockSpec((3, 4, wide), lambda g: (0, 0, g))
    return pl.pallas_call(
        functools.partial(backward_kernel, heads, passes),
        grid=(groups,),
        in_specs=[triple, fixed((length, 128)), taps, fixed((1, 128)), fixed((length, 1)), fixed((1, length))] + [block] * 5,
        out_specs=[triple, fixed((length, 128)), taps, fixed((1, 128))],
        out_shape=[
            jax.ShapeDtypeStruct((length, columns), BF16),
            jax.ShapeDtypeStruct((length, 128), F32),
            jax.ShapeDtypeStruct((3, 4, groups * wide), F32),
            jax.ShapeDtypeStruct((1, 128), F32),
        ],
        scratch_shapes=[pltpu.VMEM((length, wide), F32)] * 7,
        compiler_params=pltpu.CompilerParams(vmem_limit_bytes=56 * 2**20),
        name="mixer_backward",
    )(projected, logits, conv, gain, seg_ids[:, None], seg_ids[None, :], *saved, grad_mixed)


HEADS_PER_STEP = 2
PASSES = 3


def matmul(left, right, dims, kind=F32):
    return lax.dot_general(left, right, dims, preferred_element_type=F32).astype(kind)


def ring_order(chips):
    return [2 * i for i in range(chips // 2)] + [2 * i + 1 for i in reversed(range(chips // 2))]


def swap_tensor(value):
    return lax.ppermute(value, "tensor", [(0, 1), (1, 0)])


def pair_sum(part):
    low = part.astype(BF16)
    return low.astype(F32) + swap_tensor(low).astype(F32)


def pair_split(rows, width, core):
    blocks = rows.reshape(rows.shape[0], -1, 2, width)
    own = lax.dynamic_index_in_dim(blocks, core, 2, keepdims=False)
    other = lax.dynamic_index_in_dim(blocks, 1 - core, 2, keepdims=False)
    flat = (rows.shape[0], -1)
    return own.reshape(flat), other.reshape(flat)


def ring_scatter(own, other, chip, forward):
    chips = lax.axis_size("dp") // 2
    rows = own.shape[0] // chips
    order = ring_order(chips)
    place = [order.index(c) for c in range(chips)]
    table = jnp.asarray(order, jnp.int32)
    here = jnp.asarray(place, jnp.int32)[chip]
    turn = 1 if forward else -1
    hops = []
    for position, source in enumerate(order):
        target = order[(position + turn) % chips]
        hops += [(2 * source, 2 * target), (2 * source + 1, 2 * target + 1)]

    def local(step):
        at = table[(here - turn * (step + 1)) % chips] * rows
        a = lax.dynamic_slice_in_dim(own, at, rows, 0)
        b = lax.dynamic_slice_in_dim(other, at, rows, 0)
        return a.astype(F32) + b.astype(F32)

    total = local(0)
    for step in range(1, chips):
        moved = lax.ppermute(total.astype(BF16), "dp", hops)
        total = local(step) + moved.astype(F32)
    return total


def scatter_grads(own, other, chip, core_swap):
    other = lax.ppermute(other, "dp", core_swap)
    half = own.shape[1] // 2
    return jnp.concatenate(
        [
            ring_scatter(own[:, :half], other[:, :half], chip, True),
            ring_scatter(own[:, half:], other[:, half:], chip, False),
        ],
        axis=1,
    )


def norm_back(values, scale, gain, grad):
    scaled = gain * grad
    inner = jnp.mean(values * scaled, axis=-1, keepdims=True)
    gain_grad = jnp.sum(values * scale * grad, axis=0)
    return scale * scaled - values * (scale * scale * scale) * inner, gain_grad


def body(
    tokens,
    segments,
    cotangent,
    norm_gain,
    attn_weight,
    beta_weight,
    conv_weight,
    out_gain,
    mlp_gain,
    mlp_weight,
):
    seg_ids = segments[0]
    length = tokens.shape[0]
    devices = lax.axis_size("dp")
    index = lax.axis_index("dp")
    chip, core = index // 2, index % 2
    core_swap = [(i, i ^ 1) for i in range(devices)]
    rows, _, local_width = attn_weight.shape
    head_count = beta_weight.shape[1]
    piece = conv_weight.shape[3]
    units = mlp_weight.shape[2]
    groups = head_count // HEADS_PER_STEP
    wide = local_width // groups
    model_width = rows * devices
    taps_size = conv_weight.size

    small = jnp.concatenate(
        [norm_gain, mlp_gain, beta_weight.reshape(-1), conv_weight.reshape(-1), out_gain]
    ).astype(BF16)
    small = lax.all_gather(small, "dp", axis=0)
    attn_low = attn_weight.astype(BF16)
    qkv_local = attn_low[:, :3].reshape(rows, 3, groups, wide).transpose(0, 2, 1, 3)
    attn_local = jnp.concatenate([qkv_local.reshape(rows, 3 * local_width), attn_low[:, 3]], axis=1)
    attn_mat = lax.all_gather(attn_local, "dp", axis=0, tiled=True)
    mlp_local = mlp_weight.astype(BF16).reshape(rows, 3 * units)
    mlp_mat = lax.all_gather(mlp_local, "dp", axis=0, tiled=True)
    qkv_mat, out_mat = attn_mat[:, : 3 * local_width], attn_mat[:, 3 * local_width :]
    gu_mat, down_mat = mlp_mat[:, : 2 * units], mlp_mat[:, 2 * units :]
    at = [0, rows, 2 * rows, 2 * rows + rows * head_count]
    gain_in = small[:, at[0] : at[1]].reshape(-1).astype(F32)
    gain_mid = small[:, at[1] : at[2]].reshape(-1).astype(F32)
    beta_mat = small[:, at[2] : at[3]].reshape(model_width, head_count)
    beta_pad = jnp.pad(beta_mat, ((0, 0), (0, 128 - head_count)))
    taps = small[:, at[3] : at[3] + taps_size].reshape(devices, 3, 4, head_count, piece)
    taps = taps.transpose(1, 2, 3, 0, 4).reshape(3, 4, local_width).astype(F32)
    gain_heads = small[:, at[3] + taps_size :].reshape(1, -1).astype(F32)

    inputs_f = tokens.astype(F32)
    scale_in = lax.rsqrt(jnp.mean(inputs_f * inputs_f, axis=-1, keepdims=True) + 1e-05)
    normed = (inputs_f * scale_in * gain_in).astype(BF16)
    projected = matmul(normed, qkv_mat, NN)
    logits = matmul(normed, beta_pad, NN)
    mixed, *saved = mixer_forward(
        projected, logits, taps, gain_heads, seg_ids, HEADS_PER_STEP, PASSES
    )
    hidden = inputs_f + pair_sum(matmul(mixed, out_mat, NT))

    scale_mid = lax.rsqrt(jnp.mean(hidden * hidden, axis=-1, keepdims=True) + 1e-05)
    normed_mlp = (hidden * scale_mid * gain_mid).astype(BF16)
    gate = matmul(normed_mlp, gu_mat[:, :units], NN)
    up = matmul(normed_mlp, gu_mat[:, units:], NN)
    gate_sig = jax.nn.sigmoid(gate)
    activated = (gate * gate_sig * up).astype(BF16)
    grad_act = matmul(cotangent, down_mat, NN)
    grad_gate = (grad_act * up * gate_sig * (1.0 + gate * (1.0 - gate_sig))).astype(BF16)
    grad_up = (grad_act * gate * gate_sig).astype(BF16)
    grad_gu = jnp.concatenate([grad_gate, grad_up], axis=1)
    down = pair_sum(matmul(activated, down_mat, NT))
    result = (hidden + down).astype(BF16)

    mlp_own, mlp_other = pair_split(normed_mlp, rows, core)
    cot_own, cot_other = pair_split(cotangent, rows, core)
    grad_gu_mat = scatter_grads(
        matmul(mlp_own, grad_gu, TN, BF16), matmul(mlp_other, grad_gu, TN, BF16), chip, core_swap
    )
    grad_down_mat = scatter_grads(
        matmul(cot_own, activated, TN, BF16), matmul(cot_other, activated, TN, BF16), chip, core_swap
    )
    mlp_grad = jnp.concatenate([grad_gu_mat, grad_down_mat], axis=1).reshape(rows, 3, units)
    grad_normed_mlp = pair_sum(matmul(grad_gu, gu_mat, NT))
    grad_norm, grad_gain_mid = norm_back(hidden, scale_mid, gain_mid, grad_normed_mlp)
    grad_hidden = cotangent.astype(F32) + grad_norm
    grad_hidden_low = grad_hidden.astype(BF16)

    grad_mixed = matmul(grad_hidden_low, out_mat, NN)
    grad_proj, grad_logits, grad_taps, grad_gain_heads = mixer_backward(
        projected, logits, taps, gain_heads, seg_ids, saved, grad_mixed, HEADS_PER_STEP, PASSES
    )
    grad_logits_low = grad_logits.astype(BF16)
    hid_own, hid_other = pair_split(grad_hidden_low, rows, core)
    in_own, in_other = pair_split(normed, rows, core)
    grad_out_mat = scatter_grads(
        matmul(hid_own, mixed, TN, BF16), matmul(hid_other, mixed, TN, BF16), chip, core_swap
    )
    grad_qkv_mat = scatter_grads(
        matmul(in_own, grad_proj, TN, BF16), matmul(in_other, grad_proj, TN, BF16), chip, core_swap
    )
    grad_qkv_mat = grad_qkv_mat.reshape(rows, groups, 3, wide).transpose(0, 2, 1, 3)
    attn_grad = jnp.concatenate(
        [grad_qkv_mat.reshape(rows, 3, local_width), grad_out_mat[:, None]], axis=1
    )
    grad_beta = matmul(normed, grad_logits_low, TN)[:, :head_count]
    grad_normed = pair_sum(
        matmul(grad_proj, qkv_mat, NT) + matmul(grad_logits_low, beta_pad, NT)
    )
    grad_first, grad_gain_in = norm_back(inputs_f, scale_in, gain_in, grad_normed)
    grad_inputs = grad_hidden + grad_first

    grad_gain_heads = grad_gain_heads[0] + swap_tensor(grad_gain_heads[0])
    grad_taps = grad_taps.reshape(3, 4, head_count, devices, piece).transpose(3, 0, 1, 2, 4)
    packed = jnp.concatenate(
        [
            grad_gain_in.reshape(devices, -1),
            grad_gain_mid.reshape(devices, -1),
            grad_beta.reshape(devices, -1),
            grad_taps.reshape(devices, -1),
            grad_gain_heads.reshape(devices, -1),
        ],
        axis=1,
    )
    packed = jnp.sum(lax.all_to_all(packed, "dp", 0, 0, tiled=True), axis=0)
    return (
        result,
        grad_inputs,
        packed[at[0] : at[1]],
        attn_grad,
        packed[at[2] : at[3]].reshape(rows, head_count),
        packed[at[3] : at[3] + taps_size].reshape(conv_weight.shape),
        packed[at[3] + taps_size :],
        packed[at[1] : at[2]],
        mlp_grad,
    )


def solution(mesh):
    return jax.shard_map(
        body,
        mesh=mesh,
        in_specs=(
            P("dp", None),
            P("dp", None),
            P("dp", None),
            P("dp"),
            P("dp", None, "tensor"),
            P("dp", "tensor"),
            P(None, None, "tensor", "dp"),
            P("dp"),
            P("dp"),
            P("dp", None, "tensor"),
        ),
        out_specs=(
            P("dp", None),
            P("dp", None),
            P("dp"),
            P("dp", None, "tensor"),
            P("dp", "tensor"),
            P(None, None, "tensor", "dp"),
            P("dp"),
            P("dp"),
            P("dp", None, "tensor"),
        ),
        check_vma=False,
    )
```

```python
import functools

import jax
import jax.numpy as jnp
from jax import lax
from jax.experimental import pallas as pl
from jax.experimental.pallas import tpu as pltpu
from jax.sharding import PartitionSpec as P

F32 = jnp.float32
BF16 = jnp.bfloat16
CHUNK = 128
NN = (((1,), (0,)), ((), ()))
NT = (((1,), (1,)), ((), ()))
TN = (((0,), (0,)), ((), ()))


def split2(value):
    high = value.astype(BF16)
    return high, (value - high.astype(F32)).astype(BF16)


def dot1(left, right, dims):
    return lax.dot_general(left, right, dims, preferred_element_type=F32)


def mul3(left, right, dims):
    (lh, ll), (rh, rl) = left, right
    return dot1(lh, rh, dims) + (dot1(lh, rl, dims) + dot1(ll, rh, dims))


def mul1(left, right, dims):
    return dot1(left[0], right[0], dims)


def iotas(size):
    return (
        lax.broadcasted_iota(jnp.int32, (size, size), 0),
        lax.broadcasted_iota(jnp.int32, (size, size), 1),
    )


def allowed_rows(seg_full, offset):
    rows = lax.broadcasted_iota(jnp.int32, seg_full.shape, 0)
    earlier = pltpu.roll(seg_full, offset, 0)
    return jnp.where((earlier == seg_full) & (rows >= offset), 1.0, 0.0).astype(F32)


def conv_taps(signal, taps, gates):
    summed = signal * taps[3:4]
    for offset in range(1, 4):
        summed = summed + pltpu.roll(signal, offset, 0) * gates[offset - 1] * taps[3 - offset : 4 - offset]
    return summed


def chunk_masks(segc_ref, segr_ref, chunk):
    start = chunk * CHUNK
    col = segc_ref[start : start + CHUNK, :]
    row = segr_ref[:, start : start + CHUNK]
    same = col == row
    last = segc_ref[start + CHUNK - 1 : start + CHUNK, :]
    if chunk == 0:
        carry = jnp.zeros(col.shape, F32)
        carry_last = jnp.zeros(last.shape, F32)
    else:
        prior = segc_ref[start - 1 : start, :]
        carry = (col == prior).astype(F32)
        carry_last = (last == prior).astype(F32)
    tail = (col == last).astype(F32)
    return same, carry, carry_last, tail


def head_logits(beta_ref, head):
    lanes = lax.broadcasted_iota(jnp.int32, beta_ref.shape, 1)
    return jnp.sum(jnp.where(lanes == head, beta_ref[...], 0.0), axis=1, keepdims=True)


def forward_kernel(heads, passes, first, proj_ref, beta_ref, conv_ref, gain_ref, segc_ref, segr_ref,
                   mixed_ref, out_ref, writes_ref, solve_ref, state_ref, q_scr, k_scr, v_scr):
    group = first + pl.program_id(0)
    length = proj_ref.shape[0]
    chunks = length // CHUNK
    width = 128
    mul = mul3 if passes == 3 else mul1
    seg_full = jnp.broadcast_to(segc_ref[...], (length, width))
    gates = [allowed_rows(seg_full, offset) for offset in (1, 2, 3)]
    betas = []
    for h in range(heads):
        for which, scr in enumerate((q_scr, k_scr, v_scr)):
            column = (which * heads + h) * width
            signal = proj_ref[:, column : column + width]
            mixed_in = conv_taps(signal, conv_ref[which, :, h * width : (h + 1) * width], gates)
            value = mixed_in * jax.nn.sigmoid(mixed_in)
            if which < 2:
                value = value * lax.rsqrt(jnp.sum(value * value, axis=1, keepdims=True) + 1e-6)
            scr[:, h * width : (h + 1) * width] = value
        betas.append(jax.nn.sigmoid(head_logits(beta_ref, group * heads + h)))
    rows, cols = iotas(CHUNK)
    masks = [chunk_masks(segc_ref, segr_ref, c) for c in range(chunks)]
    items = [(h, c) for c in range(chunks) for h in range(heads)]

    def part(scr, h, c):
        return scr[c * CHUNK : (c + 1) * CHUNK, h * width : (h + 1) * width]

    def beta_of(h, c):
        return betas[h][c * CHUNK : (c + 1) * CHUNK]

    system, inverse = {}, {}
    for h, c in items:
        keys = split2(part(k_scr, h, c))
        inner = mul(keys, keys, NT)
        keep = masks[c][0] & (rows > cols)
        system[h, c] = jnp.where(keep, inner * beta_of(h, c), 0.0)
        first = (rows // 2 == cols // 2)
        inverse[h, c] = jnp.where(rows == cols, 1.0, jnp.where(first, -system[h, c], 0.0))
    size = 2
    while size < CHUNK:
        off = (rows // (2 * size) == cols // (2 * size)) & (rows // size != cols // size)
        mid = {}
        for it in items:
            step = jnp.where(off, system[it], 0.0)
            if passes == 3:
                mid[it] = mul3(split2(inverse[it]), split2(step), NN)
            else:
                mid[it] = dot1(inverse[it].astype(BF16), step.astype(BF16), NN)
        for it in items:
            if passes == 3:
                inverse[it] = inverse[it] - mul3(split2(mid[it]), split2(inverse[it]), NN)
            else:
                inverse[it] = inverse[it] - dot1(mid[it].astype(BF16), inverse[it].astype(BF16), NN)
        size *= 2
    scores, fresh, decay = {}, {}, {}
    for h, c in items:
        same, carry, carry_last, tail = masks[c]
        keys, queries, values = part(k_scr, h, c), part(q_scr, h, c), part(v_scr, h, c)
        scores[h, c] = split2(jnp.where(same & (rows >= cols), mul(split2(queries), split2(keys), NT), 0.0))
        solver = split2(inverse[h, c])
        fresh[h, c] = mul(solver, split2(values * beta_of(h, c)), NN)
        decay[h, c] = split2(mul(solver, split2(keys * (beta_of(h, c) * carry)), NN))
        solve_ref[c * CHUNK : (c + 1) * CHUNK, h * width : (h + 1) * width] = inverse[h, c]
    state = {h: jnp.zeros((width, width), F32) for h in range(heads)}
    gain = gain_ref[...]
    for c in range(chunks):
        same, carry, carry_last, tail = masks[c]
        span = slice(c * CHUNK, (c + 1) * CHUNK)
        for h in range(heads):
            state_ref[span, h * width : (h + 1) * width] = state[h]
        writes = {}
        if c == 0:
            for h in range(heads):
                writes[h] = fresh[h, c]
        else:
            split_state = {h: split2(state[h]) for h in range(heads)}
            for h in range(heads):
                writes[h] = fresh[h, c] - mul(decay[h, c], split_state[h], NN)
        for h in range(heads):
            lanes = slice(h * width, (h + 1) * width)
            writes_ref[span, lanes] = writes[h]
            result = mul(scores[h, c], split2(writes[h]), NN)
            if c > 0:
                result = result + carry * mul(split2(part(q_scr, h, c)), split_state[h], NN)
            out_ref[span, lanes] = result
            scale = lax.rsqrt(jnp.mean(result * result, axis=1, keepdims=True) + 1e-5)
            mixed_ref[span, lanes] = (result * scale * gain).astype(BF16)
        if c + 1 < chunks:
            for h in range(heads):
                add = mul(split2(part(k_scr, h, c)), split2(writes[h] * tail), TN)
                state[h] = carry_last * state[h] + add


def backward_kernel(heads, passes, first, proj_ref, beta_ref, conv_ref, gain_ref, segc_ref, segr_ref,
                    out_ref, writes_ref, solve_ref, state_ref, gmix_ref,
                    gproj_ref, gbeta_ref, gconv_ref, ggain_ref,
                    q_scr, k_scr, v_scr, gq_scr, gk_scr, gv_scr, do_scr):
    group = first + pl.program_id(0)
    length = proj_ref.shape[0]
    chunks = length // CHUNK
    width = 128
    mul = mul3 if passes == 3 else mul1
    seg_full = jnp.broadcast_to(segc_ref[...], (length, width))
    gates = [allowed_rows(seg_full, offset) for offset in (1, 2, 3)]
    gain = gain_ref[...]

    @pl.when(pl.program_id(0) == 0)
    def _():
        gbeta_ref[...] = jnp.zeros_like(gbeta_ref)
        ggain_ref[...] = jnp.zeros_like(ggain_ref)

    def convolved(which, h):
        column = (which * heads + h) * width
        signal = proj_ref[:, column : column + width]
        mixed_in = conv_taps(signal, conv_ref[which, :, h * width : (h + 1) * width], gates)
        gate = jax.nn.sigmoid(mixed_in)
        return signal, mixed_in, gate

    betas = []
    for h in range(heads):
        lanes = slice(h * width, (h + 1) * width)
        for which, scr in enumerate((q_scr, k_scr, v_scr)):
            _, mixed_in, gate = convolved(which, h)
            value = mixed_in * gate
            if which < 2:
                value = value * lax.rsqrt(jnp.sum(value * value, axis=1, keepdims=True) + 1e-6)
            scr[:, lanes] = value
        betas.append(jax.nn.sigmoid(head_logits(beta_ref, group * heads + h)))
        result, grad = out_ref[:, lanes], gmix_ref[:, lanes]
        scale = lax.rsqrt(jnp.mean(result * result, axis=1, keepdims=True) + 1e-5)
        unit = result * scale
        ggain_ref[...] += jnp.sum(unit * grad, axis=0, keepdims=True)
        scaled = grad * gain
        do_scr[:, lanes] = scale * (scaled - unit * jnp.mean(unit * scaled, axis=1, keepdims=True))
    rows, cols = iotas(CHUNK)
    masks = [chunk_masks(segc_ref, segr_ref, c) for c in range(chunks)]
    items = [(h, c) for c in range(chunks) for h in range(heads)]

    def part(scr, h, c):
        return scr[c * CHUNK : (c + 1) * CHUNK, h * width : (h + 1) * width]

    def beta_of(h, c):
        return betas[h][c * CHUNK : (c + 1) * CHUNK]

    inner, base, reach, gscore = {}, {}, {}, {}
    for h, c in items:
        same, carry, carry_last, tail = masks[c]
        keys, queries = split2(part(k_scr, h, c)), split2(part(q_scr, h, c))
        grads, writes = split2(part(do_scr, h, c)), split2(part(writes_ref, h, c))
        inner[h, c] = mul(keys, keys, NT)
        causal = same & (rows >= cols)
        scores = split2(jnp.where(causal, mul(queries, keys, NT), 0.0))
        solver = split2(part(solve_ref, h, c))
        base[h, c] = mul(solver, split2(mul(scores, grads, TN)), TN)
        if c + 1 < chunks:
            reach[h, c] = split2(mul(solver, split2(part(k_scr, h, c) * tail), TN))
        gscore = split2(jnp.where(causal, mul(grads, writes, NT), 0.0))
        gq = mul(gscore, keys, NN)
        gk = mul(gscore, queries, TN)
        span, lanes = slice(c * CHUNK, (c + 1) * CHUNK), slice(h * width, (h + 1) * width)
        if c > 0:
            gq = gq + mul(split2(part(do_scr, h, c) * carry), split2(part(state_ref, h, c)), NT)
        gq_scr[span, lanes] = gq
        gk_scr[span, lanes] = gk
    gstate = {}
    gbetas = {}
    for c in reversed(range(chunks)):
        same, carry, carry_last, tail = masks[c]
        span = slice(c * CHUNK, (c + 1) * CHUNK)
        gtarget = {}
        for h in range(heads):
            gtarget[h] = base[h, c]
            if c + 1 < chunks:
                gtarget[h] = gtarget[h] + mul(reach[h, c], split2(gstate[h]), NN)
        for h in range(heads):
            lanes = slice(h * width, (h + 1) * width)
            gk = gk_scr[span, lanes]
            keys = split2(part(k_scr, h, c))
            beta = beta_of(h, c)
            writes = part(writes_ref, h, c)
            split_target = split2(gtarget[h])
            if c + 1 < chunks:
                gk = gk + mul(split2(writes * tail), split2(gstate[h]), NT)
            strict = same & (rows > cols)
            gsys = jnp.where(strict, mul(split_target, split2(writes), NT), 0.0)
            ginner = split2(gsys * beta)
            gbeta = -jnp.sum(gsys * inner[h, c], axis=1, keepdims=True)
            gk = gk - mul(ginner, keys, NN) - mul(ginner, keys, TN)
            target = part(v_scr, h, c)
            if c > 0:
                states = split2(part(state_ref, h, c))
                target = target - carry * mul(keys, states, NN)
                grecall = gtarget[h] * (beta * carry)
                split_recall = split2(grecall)
                gk = gk - mul(split_recall, states, NT)
                new_state = mul(split2(part(q_scr, h, c)), split2(part(do_scr, h, c) * carry), TN)
                new_state = new_state - mul(keys, split_recall, TN)
                if c + 1 < chunks:
                    new_state = new_state + carry_last * gstate[h]
                gstate[h] = new_state
            gbeta = gbeta + jnp.sum(gtarget[h] * target, axis=1, keepdims=True)
            gbetas[h, c] = gbeta * beta * (1.0 - beta)
            gk_scr[span, lanes] = gk
            gv_scr[span, lanes] = gtarget[h] * beta
    for c in range(chunks):
        span = slice(c * CHUNK, (c + 1) * CHUNK)
        lane_ids = lax.broadcasted_iota(jnp.int32, (CHUNK, gbeta_ref.shape[1]), 1)
        total = gbeta_ref[span, :]
        for h in range(heads):
            total = jnp.where(lane_ids == group * heads + h, gbetas[h, c], total)
        gbeta_ref[span, :] = total
    for h in range(heads):
        lanes = slice(h * width, (h + 1) * width)
        for which, (scr, gscr) in enumerate(((q_scr, gq_scr), (k_scr, gk_scr), (v_scr, gv_scr))):
            signal, mixed_in, gate = convolved(which, h)
            grad = gscr[:, lanes]
            if which < 2:
                value = mixed_in * gate
                scale = lax.rsqrt(jnp.sum(value * value, axis=1, keepdims=True) + 1e-6)
                unit = value * scale
                grad = scale * (grad - unit * jnp.sum(unit * grad, axis=1, keepdims=True))
            grad = grad * gate * (1.0 + mixed_in * (1.0 - gate))
            taps = conv_ref[which, :, h * width : (h + 1) * width]
            gsignal = grad * taps[3:4]
            gtaps = [None] * 4
            gtaps[3] = jnp.sum(grad * signal, axis=0, keepdims=True)
            for offset in range(1, 4):
                gated = grad * gates[offset - 1]
                gtaps[3 - offset] = jnp.sum(gated * pltpu.roll(signal, offset, 0), axis=0, keepdims=True)
                gsignal = gsignal + pltpu.roll(gated, length - offset, 0) * taps[3 - offset : 4 - offset]
            gconv_ref[which, :, lanes] = jnp.concatenate(gtaps, axis=0)
            column = (which * heads + h) * width
            gproj_ref[:, column : column + width] = gsignal.astype(BF16)


def mixer_specs(length, wide, first):
    fixed = lambda shape: pl.BlockSpec(shape, lambda g: (0,) * len(shape))
    return [
        pl.BlockSpec((length, 3 * wide), lambda g: (0, g + first)),
        fixed((length, 128)),
        pl.BlockSpec((3, 4, wide), lambda g: (0, 0, g + first)),
        fixed((1, 128)),
        fixed((length, 1)),
        fixed((1, length)),
    ]


def mixer_forward(projected, logits, conv, gain, seg_ids, heads, passes, first, count):
    length = projected.shape[0]
    wide = heads * 128
    f32 = jax.ShapeDtypeStruct((length, count * wide), F32)
    block = pl.BlockSpec((length, wide), lambda g: (0, g))
    work = count * heads * length * 128
    return pl.pallas_call(
        functools.partial(forward_kernel, heads, passes, first),
        grid=(count,),
        in_specs=mixer_specs(length, wide, first),
        out_specs=[block] * 5,
        out_shape=[jax.ShapeDtypeStruct((length, count * wide), BF16), f32, f32, f32, f32],
        scratch_shapes=[pltpu.VMEM((length, wide), F32)] * 3,
        compiler_params=pltpu.CompilerParams(vmem_limit_bytes=48 * 2**20),
        cost_estimate=pl.CostEstimate(flops=work * 30000, bytes_accessed=work * 30, transcendentals=work * 4),
        name="mixer_forward",
    )(projected, logits, conv, gain, seg_ids[:, None], seg_ids[None, :])


def mixer_backward(projected, logits, conv, gain, seg_ids, saved, grad_mixed, heads, passes, first, count, base):
    length = projected.shape[0]
    wide = heads * 128
    block = pl.BlockSpec((length, wide), lambda g: (0, g + first - base))
    grads = pl.BlockSpec((length, wide), lambda g: (0, g + first))
    fixed = lambda shape: pl.BlockSpec(shape, lambda g: (0,) * len(shape))
    work = count * heads * length * 128
    return pl.pallas_call(
        functools.partial(backward_kernel, heads, passes, first),
        grid=(count,),
        in_specs=mixer_specs(length, wide, first) + [block] * 4 + [grads],
        out_specs=[
            pl.BlockSpec((length, 3 * wide), lambda g: (0, g)),
            fixed((length, 128)),
            pl.BlockSpec((3, 4, wide), lambda g: (0, 0, g)),
            fixed((1, 128)),
        ],
        out_shape=[
            jax.ShapeDtypeStruct((length, 3 * count * wide), BF16),
            jax.ShapeDtypeStruct((length, 128), F32),
            jax.ShapeDtypeStruct((3, 4, count * wide), F32),
            jax.ShapeDtypeStruct((1, 128), F32),
        ],
        scratch_shapes=[pltpu.VMEM((length, wide), F32)] * 7,
        compiler_params=pltpu.CompilerParams(vmem_limit_bytes=48 * 2**20),
        cost_estimate=pl.CostEstimate(flops=work * 60000, bytes_accessed=work * 40, transcendentals=work * 8),
        name="mixer_backward",
    )(projected, logits, conv, gain, seg_ids[:, None], seg_ids[None, :], *saved, grad_mixed)


LIMIT = 40 * 2**20


def cost(flops, *arrays):
    size = sum(a.size * a.dtype.itemsize for a in arrays)
    return pl.CostEstimate(flops=flops, bytes_accessed=size, transcendentals=0)


def whole(array):
    return pl.BlockSpec(array.shape, lambda i: (0,) * array.ndim)


def stacked(refs):
    return jnp.concatenate([ref[...] for ref in refs], axis=0)


def rows_kernel(count, left_ref, *refs):
    out_ref = refs[count]
    out_ref[...] = dot1(left_ref[...], stacked(refs[:count]), NN).astype(out_ref.dtype)


def times_rows(left, blocks, start, columns, tile, kind):
    rows = blocks[0].shape[0]
    first = start // tile
    out = jax.ShapeDtypeStruct((left.shape[0], columns), kind)
    return pl.pallas_call(
        functools.partial(rows_kernel, len(blocks)),
        grid=(columns // tile,),
        in_specs=[whole(left)]
        + [pl.BlockSpec((rows, tile), lambda i: (0, first + i)) for _ in blocks],
        out_specs=pl.BlockSpec((left.shape[0], tile), lambda i: (0, i)),
        out_shape=out,
        compiler_params=pltpu.CompilerParams(vmem_limit_bytes=LIMIT),
        cost_estimate=cost(2 * left.size * columns, left, *blocks, out),
        name="times_rows",
    )(left, *blocks)


def turned_kernel(count, extra, left_ref, *refs):
    blocks, tail = refs[:count], refs[count : count + 2 * extra]
    out_ref, total = refs[count + 2 * extra :]
    step = pl.program_id(0)

    @pl.when(step == 0)
    def _():
        total[...] = dot1(tail[0][...], tail[1][...], NT) if extra else jnp.zeros_like(total)

    total[...] += dot1(left_ref[...], stacked(blocks), NT)

    @pl.when(step == pl.num_programs(0) - 1)
    def _():
        out_ref[...] = total[...].astype(out_ref.dtype)


def times_turned(left, blocks, start, tile, kind, plane=0, planes=1, extra=()):
    rows = blocks[0].shape[0]
    first = start // tile
    length, depth = left.shape[-2:]
    each = depth // tile
    if left.ndim == 3:
        spec = pl.BlockSpec((None, length, tile), lambda i: (plane + i // each, 0, i % each))
    else:
        spec = pl.BlockSpec((length, tile), lambda i: (0, i))
    out = jax.ShapeDtypeStruct((length, rows * len(blocks)), kind)
    return pl.pallas_call(
        functools.partial(turned_kernel, len(blocks), len(extra) // 2),
        grid=(planes * each,),
        in_specs=[spec]
        + [pl.BlockSpec((rows, tile), lambda i: (0, first + i)) for _ in blocks]
        + [whole(a) for a in extra],
        out_specs=whole(out),
        out_shape=out,
        scratch_shapes=[pltpu.VMEM(out.shape, F32)],
        compiler_params=pltpu.CompilerParams(vmem_limit_bytes=LIMIT),
        cost_estimate=cost(2 * planes * length * depth * out.shape[1], left, *blocks, out),
        name="times_turned",
    )(left, *blocks, *extra)


def gated_kernel(count, normed_ref, cot_ref, *refs):
    gate_refs, up_refs, down_refs = refs[:count], refs[count : 2 * count], refs[2 * count : 3 * count]
    out_ref = refs[3 * count]
    gate = dot1(normed_ref[...], stacked(gate_refs), NN)
    up = dot1(normed_ref[...], stacked(up_refs), NN)
    grad = dot1(cot_ref[...], stacked(down_refs), NN)
    sig = jax.nn.sigmoid(gate)
    out_ref[0] = (grad * up * sig * (1.0 + gate * (1.0 - sig))).astype(BF16)
    silu = gate * sig
    out_ref[1] = (grad * silu).astype(BF16)
    out_ref[2] = (silu * up).astype(BF16)


def gated_units(normed, cot, blocks, tile):
    rows, columns = blocks[0].shape
    units = columns // 3
    each = units // tile
    length = normed.shape[0]
    out = jax.ShapeDtypeStruct((3, length, units), BF16)

    def spec(which):
        return pl.BlockSpec((rows, tile), lambda i: (0, which * each + i))

    return pl.pallas_call(
        functools.partial(gated_kernel, len(blocks)),
        grid=(each,),
        in_specs=[whole(normed), whole(cot)] + [spec(w) for w in range(3) for _ in blocks],
        out_specs=pl.BlockSpec((3, length, tile), lambda i: (0, 0, i)),
        out_shape=out,
        compiler_params=pltpu.CompilerParams(vmem_limit_bytes=LIMIT),
        cost_estimate=cost(6 * normed.size * units, normed, cot, *blocks, out),
        name="gated_units",
    )(normed, cot, *blocks, *blocks, *blocks)


def weight_kernel(split, *refs):
    out_ref, right_ref = refs[-1], refs[-2]
    if len(refs) == 3:
        out_ref[...] = dot1(refs[0][...], right_ref[...], NN).astype(BF16)
        return
    step = pl.program_id(0)

    @pl.when(step < split)
    def _():
        out_ref[...] = dot1(refs[0][...], right_ref[...], NN).astype(BF16)

    @pl.when(step >= split)
    def _():
        out_ref[...] = dot1(refs[1][...], right_ref[...], NN).astype(BF16)


def weight_grads(lefts, half, right, tile, split=0):
    features, length = lefts[0].shape
    depth = right.shape[-1]
    each = depth // tile
    if right.ndim == 3:
        columns = right.shape[0] * depth
        spec = pl.BlockSpec((None, length, tile), lambda i: (i // each, 0, i % each))
    else:
        columns = depth
        spec = pl.BlockSpec((length, tile), lambda i: (0, i))
    out = jax.ShapeDtypeStruct((features // 2, columns), BF16)
    return pl.pallas_call(
        functools.partial(weight_kernel, split // tile),
        grid=(columns // tile,),
        in_specs=[pl.BlockSpec((features // 2, length), lambda i: (half, 0)) for _ in lefts] + [spec],
        out_specs=pl.BlockSpec((features // 2, tile), lambda i: (0, i)),
        out_shape=out,
        compiler_params=pltpu.CompilerParams(vmem_limit_bytes=LIMIT),
        cost_estimate=cost(features * length * columns, lefts[0], right, out),
        name="weight_grads",
    )(*lefts, right)


def move_kernel(table_ref, in_ref, out_ref):
    out_ref[...] = in_ref[...]


def move_columns(value, table, width, inverse=False):
    length, columns = value.shape
    if width % 128:
        parts = value.reshape(length, -1, width)
        index = jnp.argsort(table) if inverse else table
        return jnp.take(parts, index, axis=1).reshape(length, columns)
    there = pl.BlockSpec((length, width), lambda i, t: (0, t[i]))
    here = pl.BlockSpec((length, width), lambda i, t: (0, i))
    return pl.pallas_call(
        move_kernel,
        grid_spec=pltpu.PrefetchScalarGridSpec(
            num_scalar_prefetch=1,
            grid=(columns // width,),
            in_specs=[here if inverse else there],
            out_specs=there if inverse else here,
        ),
        out_shape=jax.ShapeDtypeStruct(value.shape, value.dtype),
        compiler_params=pltpu.CompilerParams(vmem_limit_bytes=LIMIT),
        cost_estimate=cost(0, value, value),
        name="move_columns",
    )(table, value)


HEADS_PER_STEP = 2
PASSES = 3
PORTIONS = 4


class Box:
    def __init__(self, value):
        self.value = value


def sync(*boxes):
    values = lax.optimization_barrier(tuple(box.value for box in boxes))
    for box, value in zip(boxes, values):
        box.value = value


class Ring:
    def __init__(self, devices):
        self.chips = chips = devices // 2
        self.order = [2 * i for i in range(chips // 2)]
        self.order += [2 * i + 1 for i in reversed(range(chips // 2))]
        place = [self.order.index(c) for c in range(chips)]
        index = lax.axis_index("dp")
        chip, core = index // 2, index % 2
        here = jnp.asarray(place, jnp.int32)[chip]
        around = jnp.asarray(self.order, jnp.int32)[(here + jnp.arange(chips, dtype=jnp.int32)) % chips]
        self.table = jnp.concatenate([2 * around + core, 2 * around + 1 - core])
        self.core_swap = [(i, i ^ 1) for i in range(devices)]
        self.hops = {}
        for turn in (1, -1):
            hops = []
            for at, source in enumerate(self.order):
                target = self.order[(at + turn) % chips]
                hops += [(2 * source, 2 * target), (2 * source + 1, 2 * target + 1)]
            self.hops[turn] = hops

    def send(self, value, turn):
        return Box(lax.ppermute(value, "dp", self.hops[turn]))

    def swap(self, value):
        return Box(lax.ppermute(value, "dp", self.core_swap))

    def steps(self, portion):
        total = self.chips // 2
        return range(total * portion // PORTIONS + 1, total * (portion + 1) // PORTIONS + 1)


class Gather:
    def __init__(self, ring, own):
        self.ring = ring
        box = Box(own)
        self.blocks = {(0, 0): [box]}
        self.front = {1: box, -1: box}
        self.fresh = [((0, 0), box)]
        self.pending = [box]

    def swap(self):
        for (at, _), box in self.fresh:
            other = self.ring.swap(box.value)
            self.blocks.setdefault((at, 1), []).append(other)
            self.pending.append(other)
        self.fresh = []

    def advance(self, portion):
        chips = self.ring.chips
        for step in self.ring.steps(portion):
            for turn in (1, -1):
                value = self.front[turn].value
                if 2 * step == chips:
                    half = value.shape[1] // 2
                    value = value[:, :half] if turn == 1 else value[:, half:]
                box = self.ring.send(value, turn)
                key = (-turn * step % chips, 0)
                self.blocks.setdefault(key, []).append(box)
                self.front[turn] = box
                self.fresh.append((key, box))
                self.pending.append(box)

    def boxes(self):
        waiting, self.pending = self.pending, []
        return waiting

    def ordered(self):
        out = []
        for core in range(2):
            for at in range(self.ring.chips):
                parts = [box.value for box in self.blocks[at, core]]
                out.append(parts[0] if len(parts) == 1 else jnp.concatenate(parts, axis=1))
        most = 16
        if len(out) > most:
            many = len(out) // most
            out = [jnp.concatenate(out[i * many : (i + 1) * many], axis=0) for i in range(most)]
        return out


class Scatter:
    def __init__(self, ring, own, other):
        self.ring = ring
        self.own = Box(own)
        self.other = ring.swap(other)
        self.got = {1: None, -1: None}

    def local(self, at):
        rows = self.own.value.shape[0] // self.ring.chips
        span = slice(at * rows, (at + 1) * rows)
        return self.own.value[span].astype(F32) + self.other.value[span].astype(F32)

    def advance(self, portion):
        chips = self.ring.chips
        for step in self.ring.steps(portion):
            away = chips // 2 - step + 1
            for turn in (1, -1):
                total = self.local(turn * away % chips)
                half = total.shape[1] // 2
                if step == 1:
                    total = total[:, :half] if turn == 1 else total[:, half:]
                else:
                    got = self.got[turn].value.astype(F32)
                    if step == 2:
                        near, far = total[:, :half], total[:, half:]
                        parts = [near + got, far] if turn == 1 else [near, far + got]
                        total = jnp.concatenate(parts, axis=1)
                    else:
                        total = total + got
                self.got[turn] = self.ring.send(total.astype(BF16), turn)

    def boxes(self):
        return [box for box in self.got.values() if box is not None] + [self.own, self.other]

    def result(self):
        return self.local(0) + self.got[1].value.astype(F32) + self.got[-1].value.astype(F32)


def swap_tensor(value):
    return lax.ppermute(value, "tensor", [(0, 1), (1, 0)])


def norm_back(values, scale, gain, grad):
    scaled = gain * grad
    inner = jnp.mean(values * scaled, axis=-1, keepdims=True)
    gain_grad = jnp.sum(values * scale * grad, axis=0)
    return scale * scaled - values * (scale * scale * scale) * inner, gain_grad


def matmul(left, right, dims):
    return lax.dot_general(left, right, dims, preferred_element_type=F32)


def unit_chunks(units):
    tile = 256
    cut = (units // tile + 1) // 2 * tile
    return [(0, cut), (cut, units)]


def body(
    tokens,
    segments,
    cotangent,
    norm_gain,
    attn_weight,
    beta_weight,
    conv_weight,
    out_gain,
    mlp_gain,
    mlp_weight,
):
    seg_ids = segments[0]
    length = tokens.shape[0]
    devices = lax.axis_size("dp")
    ring = Ring(devices)
    rows, _, local_width = attn_weight.shape
    head_count = beta_weight.shape[1]
    piece = conv_weight.shape[3]
    units = mlp_weight.shape[2]
    groups = head_count // HEADS_PER_STEP
    wide = local_width // groups
    qkv = 3 * local_width
    taps_size = conv_weight.size
    chunks = unit_chunks(units)

    attn_low = attn_weight.astype(BF16)
    qkv_local = attn_low[:, :3].reshape(rows, 3, groups, wide).transpose(0, 2, 1, 3)
    attn = Gather(ring, jnp.concatenate([qkv_local.reshape(rows, qkv), attn_low[:, 3]], axis=1))
    small = Box(
        jnp.concatenate(
            [norm_gain, mlp_gain, beta_weight.reshape(-1), conv_weight.reshape(-1), out_gain]
        ).astype(BF16)
    )

    attn.advance(0)
    small.value = lax.all_gather(small.value, "dp", axis=0)
    inputs_low = Box(move_columns(tokens, ring.table, rows))
    sync(*attn.boxes(), small, inputs_low)
    attn.swap()
    attn.advance(1)
    cot = Box(move_columns(cotangent, ring.table, rows))
    cot_turned = Box(cot.value.T)
    sync(*attn.boxes(), cot, cot_turned)
    attn.swap()
    attn.advance(2)
    mlp_low = mlp_weight.astype(BF16)
    mlp = []
    for low, high in chunks:
        mlp.append(Gather(ring, mlp_low[:, :, low:high].reshape(rows, 3 * (high - low))))
    inputs_f = inputs_low.value.astype(F32)
    at = [0, rows, 2 * rows, 2 * rows + rows * head_count]
    gathered = small.value[ring.table]
    gain_in = gathered[:, at[0] : at[1]].reshape(-1).astype(F32)
    gain_mid = gathered[:, at[1] : at[2]].reshape(-1).astype(F32)
    beta_mat = gathered[:, at[2] : at[3]].reshape(devices * rows, head_count)
    beta_pad = jnp.pad(beta_mat, ((0, 0), (0, 128 - head_count)))
    taps = small.value[:, at[3] : at[3] + taps_size].reshape(devices, 3, 4, head_count, piece)
    taps = taps.transpose(1, 2, 3, 0, 4).reshape(3, 4, local_width).astype(F32)
    gain_heads = small.value[:, at[3] + taps_size :].reshape(1, -1).astype(F32)
    scale_in = lax.rsqrt(jnp.mean(inputs_f * inputs_f, axis=-1, keepdims=True) + 1e-05)
    normed = Box((inputs_f * scale_in * gain_in).astype(BF16))
    normed_turned = Box(normed.value.T)
    logits = Box(matmul(normed.value, beta_pad, NN))
    sync(*attn.boxes(), normed, normed_turned, logits, mlp[0].front[1], mlp[1].front[1])
    attn.swap()
    attn.advance(3)
    sync(*attn.boxes(), *mlp[0].boxes())

    attn.swap()
    mlp[0].advance(0)
    attn_blocks = attn.ordered()
    projected = Box(times_rows(normed.value, attn_blocks, 0, qkv, 512, F32))
    span = groups // 2
    mixers = []
    for call in range(2):
        made = mixer_forward(
            projected.value, logits.value, taps, gain_heads, seg_ids, HEADS_PER_STEP, PASSES, call * span, span
        )
        made = [Box(m) for m in made]
        mixers.append(made)
        if call == 0:
            sync(*mlp[0].boxes(), projected, *made)
            mlp[0].swap()
            mlp[0].advance(1)
    mixed = jnp.concatenate([mixers[0][0].value, mixers[1][0].value], axis=1)
    part = Box(times_turned(mixed, attn_blocks, qkv, 512, BF16))
    sync(*mlp[0].boxes(), part)
    attended = part.value.astype(F32) + swap_tensor(part.value).astype(F32)
    mlp[0].swap()
    mlp[0].advance(2)
    sync(*mlp[0].boxes())
    mlp[0].swap()
    mlp[0].advance(3)
    mlp[1].advance(0)
    sync(*mlp[0].boxes(), *mlp[1].boxes())
    mlp[0].swap()
    mlp[1].swap()
    mlp[1].advance(1)

    hidden = inputs_f + attended
    scale_mid = lax.rsqrt(jnp.mean(hidden * hidden, axis=-1, keepdims=True) + 1e-05)
    normed_mlp = (hidden * scale_mid * gain_mid).astype(BF16)
    blocks = [mlp[0].ordered()]
    acts = [Box(gated_units(normed_mlp, cot.value, blocks[0], 256))]
    mlp_turned = Box(normed_mlp.T)
    sync(*mlp[1].boxes(), acts[0], mlp_turned)
    mlp[1].swap()
    mlp[1].advance(2)

    def mlp_grads(which):
        split = 2 * acts[which].value.shape[2]
        lefts = (mlp_turned.value, cot_turned.value)
        return [Box(weight_grads(lefts, half, acts[which].value, 256, split)) for half in (0, 1)]

    own, other = mlp_grads(0)
    sync(*mlp[1].boxes(), own, other)
    mlp[1].swap()
    mlp[1].advance(3)
    sums = [Scatter(ring, own.value, other.value)]
    sync(*mlp[1].boxes(), *sums[0].boxes())
    mlp[1].swap()
    sums[0].advance(0)
    blocks.append(mlp[1].ordered())
    acts.append(Box(gated_units(normed_mlp, cot.value, blocks[1], 256)))
    sync(*sums[0].boxes(), *acts)
    sums[0].advance(1)
    parts = [
        times_turned(acts[w].value, blocks[w], 0, 256, F32, plane=0, planes=2) for w in range(2)
    ]
    part = Box((parts[0] + parts[1]).astype(BF16))
    sync(*sums[0].boxes(), part, acts[1])
    grad_normed_mlp = part.value.astype(F32) + swap_tensor(part.value).astype(F32)
    sums[0].advance(2)
    own, other = mlp_grads(1)
    sync(*sums[0].boxes(), own, other, *acts)
    sums[0].advance(3)
    sums.append(Scatter(ring, own.value, other.value))
    parts = [
        times_turned(acts[w].value, blocks[w], 2 * acts[w].value.shape[2], 256, F32, plane=2)
        for w in range(2)
    ]
    down = Box((parts[0] + parts[1]).astype(BF16))
    sync(*sums[0].boxes(), *sums[1].boxes(), down)
    sums[1].advance(0)

    grad_norm, grad_gain_mid = norm_back(hidden, scale_mid, gain_mid, grad_normed_mlp)
    grad_hidden = cot.value.astype(F32) + grad_norm
    grad_hidden_low = grad_hidden.astype(BF16)
    grad_mixed = Box(times_rows(grad_hidden_low, attn_blocks, qkv, local_width, 512, F32))
    hidden_turned = Box(grad_hidden_low.T)
    sync(*sums[1].boxes(), grad_mixed, hidden_turned, down)
    sums[1].advance(1)
    down_sum = down.value.astype(F32) + swap_tensor(down.value).astype(F32)
    result = (hidden + down_sum).astype(BF16)

    def mixer_grads(call):
        made = mixer_backward(
            projected.value,
            logits.value,
            taps,
            gain_heads,
            seg_ids,
            [m.value for m in mixers[call][1:]],
            grad_mixed.value,
            HEADS_PER_STEP,
            PASSES,
            call * span,
            span,
            call * span,
        )
        return [Box(m) for m in made]

    back = [mixer_grads(0)]
    sync(*sums[1].boxes(), back[0][0], grad_mixed)
    sums[1].advance(2)

    def attn_grads(half):
        left = weight_grads((normed_turned.value,), half, back[0][0].value, 512)
        right = weight_grads((hidden_turned.value,), half, mixed, 512)
        return Box(jnp.concatenate([left, right], axis=1))

    other, own = attn_grads(1), attn_grads(0)
    first = Scatter(ring, own.value, other.value)
    sync(*sums[1].boxes(), *first.boxes(), grad_mixed)
    sums[1].advance(3)
    first.advance(0)
    back.append(mixer_grads(1))
    sync(*sums[1].boxes(), *first.boxes(), back[1][0])
    first.advance(1)
    other, own = [Box(weight_grads((normed_turned.value,), h, back[1][0].value, 512)) for h in (1, 0)]
    second = Scatter(ring, own.value, other.value)
    grad_logits_low = (back[0][1].value + back[1][1].value).astype(BF16)
    grad_proj = jnp.concatenate([back[0][0].value, back[1][0].value], axis=1)
    part = Box(
        times_turned(grad_proj, attn_blocks, 0, 512, BF16, extra=(grad_logits_low, beta_pad))
    )
    sync(*first.boxes(), *second.boxes(), part)
    first.advance(2)
    second.advance(0)
    grad_normed = part.value.astype(F32) + swap_tensor(part.value).astype(F32)
    grad_beta = matmul(normed.value, grad_logits_low, TN)[:, :head_count]
    sync(*first.boxes(), *second.boxes())
    first.advance(3)
    second.advance(1)
    sync(*first.boxes(), *second.boxes())
    second.advance(2)
    sync(*second.boxes())
    second.advance(3)

    grad_first, grad_gain_in = norm_back(inputs_f, scale_in, gain_in, grad_normed)
    grad_inputs = grad_hidden + grad_first

    grad_gain_heads = back[0][3].value[0] + back[1][3].value[0]
    grad_gain_heads = grad_gain_heads + swap_tensor(grad_gain_heads)
    grad_taps = jnp.concatenate([back[0][2].value, back[1][2].value], axis=2)
    grad_taps = grad_taps.reshape(3, 4, head_count, devices, piece).transpose(3, 0, 1, 2, 4)
    owner = jnp.argsort(ring.table)
    by_feature = jnp.concatenate(
        [
            grad_gain_in.reshape(devices, -1),
            grad_gain_mid.reshape(devices, -1),
            grad_beta.reshape(devices, -1),
        ],
        axis=1,
    )[owner]
    packed = jnp.concatenate(
        [by_feature, grad_taps.reshape(devices, -1), grad_gain_heads.reshape(devices, -1)], axis=1
    )
    packed = jnp.sum(lax.all_to_all(packed, "dp", 0, 0, tiled=True), axis=0)

    mlp_grad = jnp.concatenate([s.result().reshape(rows, 3, -1) for s in sums], axis=2)
    first_sum, second_sum = first.result(), second.result()
    each = qkv // 2
    qkv_grad = jnp.concatenate([first_sum[:, :each], second_sum], axis=1)
    qkv_grad = qkv_grad.reshape(rows, groups, 3, wide).transpose(0, 2, 1, 3)
    attn_grad = jnp.concatenate(
        [qkv_grad.reshape(rows, 3, local_width), first_sum[:, each:][:, None]], axis=1
    )
    return (
        move_columns(result, ring.table, rows, inverse=True),
        move_columns(grad_inputs, ring.table, rows, inverse=True),
        packed[at[0] : at[1]],
        attn_grad,
        packed[at[2] : at[3]].reshape(rows, head_count),
        packed[at[3] : at[3] + taps_size].reshape(conv_weight.shape),
        packed[at[3] + taps_size :],
        packed[at[1] : at[2]],
        mlp_grad,
    )


def solution(mesh):
    return jax.shard_map(
        body,
        mesh=mesh,
        in_specs=(
            P("dp", None),
            P("dp", None),
            P("dp", None),
            P("dp"),
            P("dp", None, "tensor"),
            P("dp", "tensor"),
            P(None, None, "tensor", "dp"),
            P("dp"),
            P("dp"),
            P("dp", None, "tensor"),
        ),
        out_specs=(
            P("dp", None),
            P("dp", None),
            P("dp"),
            P("dp", None, "tensor"),
            P("dp", "tensor"),
            P(None, None, "tensor", "dp"),
            P("dp"),
            P("dp"),
            P("dp", None, "tensor"),
        ),
        check_vma=False,
    )
```

```python
import functools

import jax
import jax.numpy as jnp
from jax import lax
from jax.experimental import pallas as pl
from jax.experimental.pallas import tpu as pltpu
from jax.sharding import PartitionSpec as P

F32 = jnp.float32
BF16 = jnp.bfloat16
CHUNK = 128
NN = (((1,), (0,)), ((), ()))
NT = (((1,), (1,)), ((), ()))
TN = (((0,), (0,)), ((), ()))


def split2(value):
    high = value.astype(BF16)
    return high, (value - high.astype(F32)).astype(BF16)


def dot1(left, right, dims):
    return lax.dot_general(left, right, dims, preferred_element_type=F32)


def mul3(left, right, dims):
    (lh, ll), (rh, rl) = left, right
    return dot1(lh, rh, dims) + (dot1(lh, rl, dims) + dot1(ll, rh, dims))


def mul1(left, right, dims):
    return dot1(left[0], right[0], dims)


def iotas(size):
    return (
        lax.broadcasted_iota(jnp.int32, (size, size), 0),
        lax.broadcasted_iota(jnp.int32, (size, size), 1),
    )


def allowed_rows(seg_full, offset):
    rows = lax.broadcasted_iota(jnp.int32, seg_full.shape, 0)
    earlier = pltpu.roll(seg_full, offset, 0)
    return jnp.where((earlier == seg_full) & (rows >= offset), 1.0, 0.0).astype(F32)


def conv_taps(signal, taps, gates):
    summed = signal * taps[3:4]
    for offset in range(1, 4):
        summed = summed + pltpu.roll(signal, offset, 0) * gates[offset - 1] * taps[3 - offset : 4 - offset]
    return summed


def chunk_masks(segc_ref, segr_ref, chunk):
    start = chunk * CHUNK
    col = segc_ref[start : start + CHUNK, :]
    row = segr_ref[:, start : start + CHUNK]
    same = col == row
    last = segc_ref[start + CHUNK - 1 : start + CHUNK, :]
    if chunk == 0:
        carry = jnp.zeros(col.shape, F32)
        carry_last = jnp.zeros(last.shape, F32)
    else:
        prior = segc_ref[start - 1 : start, :]
        carry = (col == prior).astype(F32)
        carry_last = (last == prior).astype(F32)
    tail = (col == last).astype(F32)
    return same, carry, carry_last, tail


def head_logits(beta_ref, head):
    lanes = lax.broadcasted_iota(jnp.int32, beta_ref.shape, 1)
    return jnp.sum(jnp.where(lanes == head, beta_ref[...], 0.0), axis=1, keepdims=True)


def forward_kernel(heads, passes, first, proj_ref, beta_ref, conv_ref, gain_ref, segc_ref, segr_ref,
                   mixed_ref, out_ref, writes_ref, solve_ref, state_ref, q_scr, k_scr, v_scr):
    group = first + pl.program_id(0)
    length = proj_ref.shape[0]
    chunks = length // CHUNK
    width = 128
    mul = mul3 if passes == 3 else mul1
    seg_full = jnp.broadcast_to(segc_ref[...], (length, width))
    gates = [allowed_rows(seg_full, offset) for offset in (1, 2, 3)]
    betas = []
    for h in range(heads):
        for which, scr in enumerate((q_scr, k_scr, v_scr)):
            column = (which * heads + h) * width
            signal = proj_ref[:, column : column + width]
            mixed_in = conv_taps(signal, conv_ref[which, :, h * width : (h + 1) * width], gates)
            value = mixed_in * jax.nn.sigmoid(mixed_in)
            if which < 2:
                value = value * lax.rsqrt(jnp.sum(value * value, axis=1, keepdims=True) + 1e-6)
            scr[:, h * width : (h + 1) * width] = value
        betas.append(jax.nn.sigmoid(head_logits(beta_ref, group * heads + h)))
    rows, cols = iotas(CHUNK)
    masks = [chunk_masks(segc_ref, segr_ref, c) for c in range(chunks)]
    items = [(h, c) for c in range(chunks) for h in range(heads)]

    def part(scr, h, c):
        return scr[c * CHUNK : (c + 1) * CHUNK, h * width : (h + 1) * width]

    def beta_of(h, c):
        return betas[h][c * CHUNK : (c + 1) * CHUNK]

    system, inverse = {}, {}
    for h, c in items:
        keys = split2(part(k_scr, h, c))
        inner = mul(keys, keys, NT)
        keep = masks[c][0] & (rows > cols)
        system[h, c] = jnp.where(keep, inner * beta_of(h, c), 0.0)
        first = (rows // 2 == cols // 2)
        inverse[h, c] = jnp.where(rows == cols, 1.0, jnp.where(first, -system[h, c], 0.0))
    size = 2
    while size < CHUNK:
        off = (rows // (2 * size) == cols // (2 * size)) & (rows // size != cols // size)
        mid = {}
        for it in items:
            step = jnp.where(off, system[it], 0.0)
            if passes == 3:
                mid[it] = mul3(split2(inverse[it]), split2(step), NN)
            else:
                mid[it] = dot1(inverse[it].astype(BF16), step.astype(BF16), NN)
        for it in items:
            if passes == 3:
                inverse[it] = inverse[it] - mul3(split2(mid[it]), split2(inverse[it]), NN)
            else:
                inverse[it] = inverse[it] - dot1(mid[it].astype(BF16), inverse[it].astype(BF16), NN)
        size *= 2
    scores, fresh, decay = {}, {}, {}
    for h, c in items:
        same, carry, carry_last, tail = masks[c]
        keys, queries, values = part(k_scr, h, c), part(q_scr, h, c), part(v_scr, h, c)
        scores[h, c] = split2(jnp.where(same & (rows >= cols), mul(split2(queries), split2(keys), NT), 0.0))
        solver = split2(inverse[h, c])
        fresh[h, c] = mul(solver, split2(values * beta_of(h, c)), NN)
        decay[h, c] = split2(mul(solver, split2(keys * (beta_of(h, c) * carry)), NN))
        solve_ref[c * CHUNK : (c + 1) * CHUNK, h * width : (h + 1) * width] = inverse[h, c]
    state = {h: jnp.zeros((width, width), F32) for h in range(heads)}
    gain = gain_ref[...]
    for c in range(chunks):
        same, carry, carry_last, tail = masks[c]
        span = slice(c * CHUNK, (c + 1) * CHUNK)
        for h in range(heads):
            state_ref[span, h * width : (h + 1) * width] = state[h]
        writes = {}
        if c == 0:
            for h in range(heads):
                writes[h] = fresh[h, c]
        else:
            split_state = {h: split2(state[h]) for h in range(heads)}
            for h in range(heads):
                writes[h] = fresh[h, c] - mul(decay[h, c], split_state[h], NN)
        for h in range(heads):
            lanes = slice(h * width, (h + 1) * width)
            writes_ref[span, lanes] = writes[h]
            result = mul(scores[h, c], split2(writes[h]), NN)
            if c > 0:
                result = result + carry * mul(split2(part(q_scr, h, c)), split_state[h], NN)
            out_ref[span, lanes] = result
            scale = lax.rsqrt(jnp.mean(result * result, axis=1, keepdims=True) + 1e-5)
            mixed_ref[span, lanes] = (result * scale * gain).astype(BF16)
        if c + 1 < chunks:
            for h in range(heads):
                add = mul(split2(part(k_scr, h, c)), split2(writes[h] * tail), TN)
                state[h] = carry_last * state[h] + add


def backward_kernel(heads, passes, first, proj_ref, beta_ref, conv_ref, gain_ref, segc_ref, segr_ref,
                    out_ref, writes_ref, solve_ref, state_ref, gmix_ref,
                    gproj_ref, gbeta_ref, gconv_ref, ggain_ref,
                    q_scr, k_scr, v_scr, gq_scr, gk_scr, gv_scr, do_scr):
    group = first + pl.program_id(0)
    length = proj_ref.shape[0]
    chunks = length // CHUNK
    width = 128
    mul = mul3 if passes == 3 else mul1
    seg_full = jnp.broadcast_to(segc_ref[...], (length, width))
    gates = [allowed_rows(seg_full, offset) for offset in (1, 2, 3)]
    gain = gain_ref[...]

    @pl.when(pl.program_id(0) == 0)
    def _():
        gbeta_ref[...] = jnp.zeros_like(gbeta_ref)
        ggain_ref[...] = jnp.zeros_like(ggain_ref)

    def convolved(which, h):
        column = (which * heads + h) * width
        signal = proj_ref[:, column : column + width]
        mixed_in = conv_taps(signal, conv_ref[which, :, h * width : (h + 1) * width], gates)
        gate = jax.nn.sigmoid(mixed_in)
        return signal, mixed_in, gate

    betas = []
    for h in range(heads):
        lanes = slice(h * width, (h + 1) * width)
        for which, scr in enumerate((q_scr, k_scr, v_scr)):
            _, mixed_in, gate = convolved(which, h)
            value = mixed_in * gate
            if which < 2:
                value = value * lax.rsqrt(jnp.sum(value * value, axis=1, keepdims=True) + 1e-6)
            scr[:, lanes] = value
        betas.append(jax.nn.sigmoid(head_logits(beta_ref, group * heads + h)))
        result, grad = out_ref[:, lanes], gmix_ref[:, lanes]
        scale = lax.rsqrt(jnp.mean(result * result, axis=1, keepdims=True) + 1e-5)
        unit = result * scale
        ggain_ref[...] += jnp.sum(unit * grad, axis=0, keepdims=True)
        scaled = grad * gain
        do_scr[:, lanes] = scale * (scaled - unit * jnp.mean(unit * scaled, axis=1, keepdims=True))
    rows, cols = iotas(CHUNK)
    masks = [chunk_masks(segc_ref, segr_ref, c) for c in range(chunks)]
    items = [(h, c) for c in range(chunks) for h in range(heads)]

    def part(scr, h, c):
        return scr[c * CHUNK : (c + 1) * CHUNK, h * width : (h + 1) * width]

    def beta_of(h, c):
        return betas[h][c * CHUNK : (c + 1) * CHUNK]

    inner, base, reach, gscore = {}, {}, {}, {}
    for h, c in items:
        same, carry, carry_last, tail = masks[c]
        keys, queries = split2(part(k_scr, h, c)), split2(part(q_scr, h, c))
        grads, writes = split2(part(do_scr, h, c)), split2(part(writes_ref, h, c))
        inner[h, c] = mul(keys, keys, NT)
        causal = same & (rows >= cols)
        scores = split2(jnp.where(causal, mul(queries, keys, NT), 0.0))
        solver = split2(part(solve_ref, h, c))
        base[h, c] = mul(solver, split2(mul(scores, grads, TN)), TN)
        if c + 1 < chunks:
            reach[h, c] = split2(mul(solver, split2(part(k_scr, h, c) * tail), TN))
        gscore = split2(jnp.where(causal, mul(grads, writes, NT), 0.0))
        gq = mul(gscore, keys, NN)
        gk = mul(gscore, queries, TN)
        span, lanes = slice(c * CHUNK, (c + 1) * CHUNK), slice(h * width, (h + 1) * width)
        if c > 0:
            gq = gq + mul(split2(part(do_scr, h, c) * carry), split2(part(state_ref, h, c)), NT)
        gq_scr[span, lanes] = gq
        gk_scr[span, lanes] = gk
    gstate = {}
    gbetas = {}
    for c in reversed(range(chunks)):
        same, carry, carry_last, tail = masks[c]
        span = slice(c * CHUNK, (c + 1) * CHUNK)
        gtarget = {}
        for h in range(heads):
            gtarget[h] = base[h, c]
            if c + 1 < chunks:
                gtarget[h] = gtarget[h] + mul(reach[h, c], split2(gstate[h]), NN)
        for h in range(heads):
            lanes = slice(h * width, (h + 1) * width)
            gk = gk_scr[span, lanes]
            keys = split2(part(k_scr, h, c))
            beta = beta_of(h, c)
            writes = part(writes_ref, h, c)
            split_target = split2(gtarget[h])
            if c + 1 < chunks:
                gk = gk + mul(split2(writes * tail), split2(gstate[h]), NT)
            strict = same & (rows > cols)
            gsys = jnp.where(strict, mul(split_target, split2(writes), NT), 0.0)
            ginner = split2(gsys * beta)
            gbeta = -jnp.sum(gsys * inner[h, c], axis=1, keepdims=True)
            gk = gk - mul(ginner, keys, NN) - mul(ginner, keys, TN)
            target = part(v_scr, h, c)
            if c > 0:
                states = split2(part(state_ref, h, c))
                target = target - carry * mul(keys, states, NN)
                grecall = gtarget[h] * (beta * carry)
                split_recall = split2(grecall)
                gk = gk - mul(split_recall, states, NT)
                new_state = mul(split2(part(q_scr, h, c)), split2(part(do_scr, h, c) * carry), TN)
                new_state = new_state - mul(keys, split_recall, TN)
                if c + 1 < chunks:
                    new_state = new_state + carry_last * gstate[h]
                gstate[h] = new_state
            gbeta = gbeta + jnp.sum(gtarget[h] * target, axis=1, keepdims=True)
            gbetas[h, c] = gbeta * beta * (1.0 - beta)
            gk_scr[span, lanes] = gk
            gv_scr[span, lanes] = gtarget[h] * beta
    for c in range(chunks):
        span = slice(c * CHUNK, (c + 1) * CHUNK)
        lane_ids = lax.broadcasted_iota(jnp.int32, (CHUNK, gbeta_ref.shape[1]), 1)
        total = gbeta_ref[span, :]
        for h in range(heads):
            total = jnp.where(lane_ids == group * heads + h, gbetas[h, c], total)
        gbeta_ref[span, :] = total
    for h in range(heads):
        lanes = slice(h * width, (h + 1) * width)
        for which, (scr, gscr) in enumerate(((q_scr, gq_scr), (k_scr, gk_scr), (v_scr, gv_scr))):
            signal, mixed_in, gate = convolved(which, h)
            grad = gscr[:, lanes]
            if which < 2:
                value = mixed_in * gate
                scale = lax.rsqrt(jnp.sum(value * value, axis=1, keepdims=True) + 1e-6)
                unit = value * scale
                grad = scale * (grad - unit * jnp.sum(unit * grad, axis=1, keepdims=True))
            grad = grad * gate * (1.0 + mixed_in * (1.0 - gate))
            taps = conv_ref[which, :, h * width : (h + 1) * width]
            gsignal = grad * taps[3:4]
            gtaps = [None] * 4
            gtaps[3] = jnp.sum(grad * signal, axis=0, keepdims=True)
            for offset in range(1, 4):
                gated = grad * gates[offset - 1]
                gtaps[3 - offset] = jnp.sum(gated * pltpu.roll(signal, offset, 0), axis=0, keepdims=True)
                gsignal = gsignal + pltpu.roll(gated, length - offset, 0) * taps[3 - offset : 4 - offset]
            gconv_ref[which, :, lanes] = jnp.concatenate(gtaps, axis=0)
            column = (which * heads + h) * width
            gproj_ref[:, column : column + width] = gsignal.astype(BF16)


def mixer_specs(length, wide, first):
    fixed = lambda shape: pl.BlockSpec(shape, lambda g: (0,) * len(shape))
    return [
        pl.BlockSpec((length, 3 * wide), lambda g: (0, g + first)),
        fixed((length, 128)),
        pl.BlockSpec((3, 4, wide), lambda g: (0, 0, g + first)),
        fixed((1, 128)),
        fixed((length, 1)),
        fixed((1, length)),
    ]


def mixer_forward(projected, logits, conv, gain, seg_ids, heads, passes, first, count):
    length = projected.shape[0]
    wide = heads * 128
    f32 = jax.ShapeDtypeStruct((length, count * wide), F32)
    block = pl.BlockSpec((length, wide), lambda g: (0, g))
    return pl.pallas_call(
        functools.partial(forward_kernel, heads, passes, first),
        grid=(count,),
        in_specs=mixer_specs(length, wide, first),
        out_specs=[block] * 5,
        out_shape=[jax.ShapeDtypeStruct((length, count * wide), BF16), f32, f32, f32, f32],
        scratch_shapes=[pltpu.VMEM((length, wide), F32)] * 3,
        compiler_params=pltpu.CompilerParams(vmem_limit_bytes=48 * 2**20),
        cost_estimate=pl.CostEstimate(flops=1000, bytes_accessed=1000, transcendentals=0),
        name="mixer_forward",
    )(projected, logits, conv, gain, seg_ids[:, None], seg_ids[None, :])


def mixer_backward(projected, logits, conv, gain, seg_ids, saved, grad_mixed, heads, passes, first, count, base):
    length = projected.shape[0]
    wide = heads * 128
    block = pl.BlockSpec((length, wide), lambda g: (0, g + first - base))
    grads = pl.BlockSpec((length, wide), lambda g: (0, g + first))
    fixed = lambda shape: pl.BlockSpec(shape, lambda g: (0,) * len(shape))
    return pl.pallas_call(
        functools.partial(backward_kernel, heads, passes, first),
        grid=(count,),
        in_specs=mixer_specs(length, wide, first) + [block] * 4 + [grads],
        out_specs=[
            pl.BlockSpec((length, 3 * wide), lambda g: (0, g)),
            fixed((length, 128)),
            pl.BlockSpec((3, 4, wide), lambda g: (0, 0, g)),
            fixed((1, 128)),
        ],
        out_shape=[
            jax.ShapeDtypeStruct((length, 3 * count * wide), BF16),
            jax.ShapeDtypeStruct((length, 128), F32),
            jax.ShapeDtypeStruct((3, 4, count * wide), F32),
            jax.ShapeDtypeStruct((1, 128), F32),
        ],
        scratch_shapes=[pltpu.VMEM((length, wide), F32)] * 7,
        compiler_params=pltpu.CompilerParams(vmem_limit_bytes=48 * 2**20),
        cost_estimate=pl.CostEstimate(flops=1000, bytes_accessed=1000, transcendentals=0),
        name="mixer_backward",
    )(projected, logits, conv, gain, seg_ids[:, None], seg_ids[None, :], *saved, grad_mixed)


LIMIT = 48 * 2**20


def whole(array):
    return pl.BlockSpec(array.shape, lambda *_: (0,) * array.ndim)


def call(kernel, grid, in_specs, out_specs, out_shape, name, table, *operands, scratch=()):
    return pl.pallas_call(
        kernel,
        grid_spec=pltpu.PrefetchScalarGridSpec(
            num_scalar_prefetch=1,
            grid=grid,
            in_specs=in_specs,
            out_specs=out_specs,
            scratch_shapes=scratch,
        ),
        out_shape=out_shape,
        compiler_params=pltpu.CompilerParams(vmem_limit_bytes=LIMIT),
        cost_estimate=pl.CostEstimate(flops=1000, bytes_accessed=1000, transcendentals=0),
        name=name,
    )(table, *operands)


IN_PLACE = pl.BlockSpec(memory_space=pl.ANY)


def lanes_at(place, width):
    return pl.ds(pl.multiple_of(place * width, width), width)


def column_tiles(blocks, starts, tile, table_ref, hold, sems):
    rows = blocks[0].shape[0]
    step, count = pl.program_id(0), pl.num_programs(0)

    def copies(at):
        slot = lax.rem(at, 2)
        for w, start in enumerate(starts):
            columns = pl.ds(pl.multiple_of(start + at * tile, 128), tile)
            for r, block in enumerate(blocks):
                yield pltpu.make_async_copy(
                    block.at[:, columns],
                    hold.at[slot, w, lanes_at(table_ref[r], rows), :],
                    sems.at[slot, w, r],
                )

    @pl.when(step == 0)
    def _():
        for copy in copies(step):
            copy.start()

    @pl.when(step + 1 < count)
    def _():
        for copy in copies(step + 1):
            copy.start()

    for copy in copies(step):
        copy.wait()
    return lax.rem(step, 2)


def tile_scratch(blocks, ranges, tile):
    rows, count = blocks[0].shape[0], len(blocks)
    return [
        pltpu.VMEM((2, ranges, rows * count, tile), BF16),
        pltpu.SemaphoreType.DMA((2, ranges, count)),
    ]


def rows_kernel(count, start, tile, table_ref, left_ref, *refs):
    blocks, (out_ref, hold, sems) = refs[:count], refs[count:]
    slot = column_tiles(blocks, [start], tile, table_ref, hold, sems)
    out_ref[...] = dot1(left_ref[...], hold[slot, 0], NN).astype(out_ref.dtype)


def times_rows(left, blocks, table, start, columns, tile, kind):
    return call(
        functools.partial(rows_kernel, len(blocks), start, tile),
        (columns // tile,),
        [whole(left)] + [IN_PLACE] * len(blocks),
        pl.BlockSpec((left.shape[0], tile), lambda i, t: (0, i)),
        jax.ShapeDtypeStruct((left.shape[0], columns), kind),
        "times_rows",
        table,
        left,
        *blocks,
        scratch=tile_scratch(blocks, 1, tile),
    )


def gated_kernel(table_ref, normed_ref, cot_ref, gate_ref, up_ref, down_ref, out_ref):
    gate = dot1(normed_ref[...], gate_ref[...], NN)
    up = dot1(normed_ref[...], up_ref[...], NN)
    grad = dot1(cot_ref[...], down_ref[...], NN)
    sig = jax.nn.sigmoid(gate)
    silu = gate * sig
    out_ref[0] = (grad * up * sig * (1.0 + gate * (1.0 - sig))).astype(BF16)
    out_ref[1] = (grad * silu).astype(BF16)
    out_ref[2] = (silu * up).astype(BF16)


def gated_units(normed, cot, mat, table, tile):
    width, columns = mat.shape
    units = columns // 3
    each = units // tile
    length = normed.shape[0]

    def spec(which):
        return pl.BlockSpec((width, tile), lambda i, t: (0, which * each + i))

    return call(
        gated_kernel,
        (each,),
        [whole(normed), whole(cot)] + [spec(w) for w in range(3)],
        pl.BlockSpec((3, length, tile), lambda i, t: (0, 0, i)),
        jax.ShapeDtypeStruct((3, length, units), BF16),
        "gated_units",
        table,
        normed,
        cot,
        mat,
        mat,
        mat,
    )


def units_kernel(terms, plus, table_ref, *refs):
    out_ref = refs[-1]
    total = refs[2 * terms][...] if plus else None
    for n in range(terms):
        part = dot1(refs[n][...], refs[terms + n][...], NT)
        total = part if total is None else total + part
    out_ref[...] = total.astype(out_ref.dtype)


def units_turned(terms, tile, kind, table, plus=None):
    acts, mats, act_specs, mat_specs = [], [], [], []
    for act, plane, mat in terms:
        length, units = act.shape[1:]
        width = mat.shape[0]
        acts.append(act)
        mats.append(mat)
        act_specs.append(pl.BlockSpec((None, length, units), lambda i, t, p=plane: (p, 0, 0)))
        mat_specs.append(pl.BlockSpec((tile, units), lambda i, t, p=plane: (i, p)))
    column = pl.BlockSpec((length, tile), lambda i, t: (0, i))
    more = [] if plus is None else [plus]
    return call(
        functools.partial(units_kernel, len(terms), len(more)),
        (width // tile,),
        act_specs + mat_specs + [column for _ in more],
        column,
        jax.ShapeDtypeStruct((length, width), kind),
        "units_turned",
        table,
        *acts,
        *mats,
        *more,
    )


def turned_kernel(plan, extra, table_ref, *refs):
    lefts = refs[: sum(len(pieces) for _, _, _, pieces in plan)]
    refs = refs[len(lefts) :]
    blocks = []
    for count, _, _, _ in plan:
        blocks.append(refs[:count])
        refs = refs[count:]
    tail, refs = refs[:extra], refs[extra:]
    out_ref, sems, holds = refs[0], refs[1], refs[2:]
    step, last = pl.program_id(0), pl.num_programs(0) - 1
    rows = blocks[0][0].shape[0]
    count = len(blocks[0])

    def copies(r):
        for g, (_, start, width, _) in enumerate(plan):
            yield pltpu.make_async_copy(
                blocks[g][r].at[:, start : start + width],
                holds[g].at[r // 2 % 2, r % 2 * rows : (r % 2 + 1) * rows, :],
                sems.at[g, r // 2 % 2, r % 2],
            )

    for r in range(count):
        if r < 2:

            @pl.when(step == 0)
            def _():
                for copy in copies(r):
                    copy.start()

        else:

            @pl.when(step + 1 == r // 2)
            def _():
                for copy in copies(r):
                    copy.start()

    for r in range(count):

        @pl.when(step == r // 2)
        def _():
            for copy in copies(r):
                copy.wait()

    slot = lax.rem(step, 2)
    total, at = None, 0
    for g, (_, _, _, pieces) in enumerate(plan):
        low = 0
        for plane in pieces:
            left = lefts[at][plane] if plane is not None else lefts[at][...]
            high = low + left.shape[1]
            part = dot1(left, holds[g][slot, :, low:high], NT)
            total = part if total is None else total + part
            low, at = high, at + 1
    for k in range(2):
        place = table_ref[2 * step + k]
        piece = total[:, k * rows : (k + 1) * rows]
        if extra:
            piece = piece + dot1(tail[0][...], tail[1][lanes_at(place, rows), :], NT)
        out_ref[:, lanes_at(place, rows)] = piece.astype(BF16)


def times_turned(groups, table, extra=()):
    plan, lefts, left_specs, blocks = [], [], [], []
    for pieces, own_blocks, start in groups:
        width, planes = 0, []
        for piece in pieces:
            if isinstance(piece, tuple):
                piece, plane = piece
                planes.append(0)
                left_specs.append(
                    pl.BlockSpec((1,) + piece.shape[1:], lambda i, t, plane=plane: (plane, 0, 0))
                )
            else:
                planes.append(None)
                left_specs.append(whole(piece))
            lefts.append(piece)
            width += piece.shape[-1]
        plan.append((len(own_blocks), start, width, planes))
        blocks += own_blocks
    rows, count = groups[0][1][0].shape[0], plan[0][0]
    length = lefts[0].shape[-2]
    out = jax.ShapeDtypeStruct((length, rows * count), BF16)
    return call(
        functools.partial(turned_kernel, plan, len(extra)),
        (count // 2,),
        left_specs + [IN_PLACE] * len(blocks) + [whole(a) for a in extra],
        whole(out),
        out,
        "times_turned",
        table,
        *lefts,
        *blocks,
        *extra,
        scratch=[pltpu.SemaphoreType.DMA((len(plan), 2, 2))]
        + [pltpu.VMEM((2, 2 * rows, width), BF16) for _, _, width, _ in plan],
    )


def weight_kernel(cuts, which, plus, table_ref, *refs):
    pairs = len(cuts) - 1
    lefts, rights, out_ref, turned = refs[:pairs], refs[pairs : 2 * pairs], refs[-2], refs[-1]
    step = pl.program_id(0)
    block = 128
    for n in range(pairs):

        @pl.when(step == cuts[n])
        def _():
            for at in range(turned.shape[0] // block):
                if which is None:
                    lanes = slice(at * block, (at + 1) * block)
                else:
                    lanes = lanes_at(2 * at + table_ref[which], block)
                turned[at * block : (at + 1) * block, :] = lefts[n][:, lanes].T

        @pl.when((step >= cuts[n]) & (step < cuts[n + 1]))
        def _():
            product = dot1(turned[...], rights[n][...], NN)
            if plus:
                product = product + refs[2 * pairs][...].reshape(product.shape).astype(F32)
            out_ref[...] = product.astype(BF16).reshape(out_ref.shape)


def weight_grads(pairs, tile, rows, cores, which, plus=None):
    length, features = pairs[0][0].shape
    chips = features // (2 * rows)
    inside = rows % 128 == 0
    cuts, lefts, rights, specs = [0], [], [], []
    for left, right, plane, planes in pairs:
        if not inside:
            left = left.reshape(length, chips, 2, rows)
            left = lax.dynamic_index_in_dim(left, cores[which], 2, keepdims=False)
            left = left.reshape(length, chips * rows)
        each = right.shape[-1] // tile
        low, most = cuts[-1], planes * each - 1
        if right.ndim == 3:
            spec = pl.BlockSpec(
                (None, length, tile),
                lambda i, t, low=low, most=most, plane=plane, each=each: (
                    plane + jnp.clip(i - low, 0, most) // each,
                    0,
                    jnp.clip(i - low, 0, most) % each,
                ),
            )
        else:
            spec = pl.BlockSpec(
                (length, tile), lambda i, t, low=low, most=most: (0, jnp.clip(i - low, 0, most))
            )
        lefts.append(left)
        rights.append(right)
        specs.append(spec)
        cuts.append(low + most + 1)
    place = pl.BlockSpec((chips, rows, tile), lambda i, t: (0, 0, i))
    more = [] if plus is None else [plus]
    return call(
        functools.partial(weight_kernel, cuts, which if inside else None, len(more)),
        (cuts[-1],),
        [whole(left) for left in lefts] + specs + [place for _ in more],
        place,
        jax.ShapeDtypeStruct((chips, rows, cuts[-1] * tile), BF16),
        "weight_grads",
        cores,
        *lefts,
        *rights,
        *more,
        scratch=[pltpu.VMEM((chips * rows, length), BF16)],
    )


def hop_tile(half):
    for parts in (2, 3, 1):
        if half % (128 * parts) == 0:
            return half // parts
    return 128


def hop_kernel(kind, each, table_ref, *refs):
    step = pl.program_id(0)
    for d in range(2):
        total = refs[d][...]
        if kind == "first":
            refs[2 + d][...] = total
        elif kind == "middle":
            refs[4 + d][...] = (total.astype(F32) + refs[2 + d][...].astype(F32)).astype(BF16)
        else:
            mine = (step < each) if d == 0 else (step >= each)

            @pl.when(mine)
            def _():
                refs[4 + d][...] = (total.astype(F32) + refs[2 + d][...].astype(F32)).astype(BF16)

            @pl.when(jnp.logical_not(mine))
            def _():
                refs[4 + d][...] = total


def ring_hop(kind, own, got, table, ahead, behind):
    chips, rows, columns = own.shape
    half = columns // 2
    tile = hop_tile(half)
    each = half // tile

    def term(place, offset=0):
        return pl.BlockSpec((None, rows, tile), lambda i, t: (t[place], 0, i + offset))

    flat = pl.BlockSpec((rows, tile), lambda i, t: (0, i))
    if kind == "first":
        specs = [term(ahead), term(behind, each)]
        steps, width = each, half
    else:
        specs = [term(ahead), term(behind)]
        steps, width = 2 * each, columns
        if kind == "middle":
            specs += [flat, flat]
        else:
            specs += [
                pl.BlockSpec((rows, tile), lambda i, t: (0, jnp.minimum(i, each - 1))),
                pl.BlockSpec((rows, tile), lambda i, t: (0, jnp.maximum(i - each, 0))),
            ]
    return call(
        functools.partial(hop_kernel, kind, each),
        (steps,),
        specs,
        [flat, flat],
        [jax.ShapeDtypeStruct((rows, width), BF16)] * 2,
        "ring_hop",
        table,
        own,
        own,
        *got,
    )


def landed(refs):
    return refs[0][...].astype(F32) + refs[1][...].astype(F32) + refs[2][...].astype(F32)


def units_result_kernel(table_ref, *refs):
    low = 0
    for n in range(0, len(refs) - 1, 3):
        total = landed(refs[n : n + 3])
        refs[-1][:, low : low + total.shape[1]] = total
        low += total.shape[1]


def units_result(sums, table):
    operands, specs, units = [], [], 0
    for own, ahead, behind in sums:
        _, rows, columns = own.shape
        units += columns // 3
        term = pl.BlockSpec((None, rows, columns // 3), lambda i, t: (t[0], 0, i))
        flat = pl.BlockSpec((rows, columns // 3), lambda i, t: (0, i))
        operands += [own, ahead, behind]
        specs += [term, flat, flat]
    return call(
        units_result_kernel,
        (3,),
        specs,
        pl.BlockSpec((None, rows, units), lambda i, t: (i, 0, 0)),
        jax.ShapeDtypeStruct((3, rows, units), F32),
        "units_result",
        table,
        *operands,
    )


def mixer_result_kernel(wide, table_ref, *refs):
    out_ref = refs[-1]
    group = 0
    for n in range(0, len(refs) - 1, 3):
        total = landed(refs[n : n + 3])
        columns = total.shape[1]
        low = 0
        while columns - low >= 3 * wide and (n > 0 or columns - low > out_ref.shape[2]):
            for p in range(3):
                out_ref[:, p, group * wide : (group + 1) * wide] = total[:, low : low + wide]
                low += wide
            group += 1
        if low < columns:
            out_ref[:, 3, :] = total[:, low:]


def mixer_result(sums, wide, local_width, table):
    operands, specs = [], []
    step = 32
    for own, ahead, behind in sums:
        _, rows, columns = own.shape
        term = pl.BlockSpec((None, step, columns), lambda i, t: (t[0], i, 0))
        flat = pl.BlockSpec((step, columns), lambda i, t: (i, 0))
        operands += [own, ahead, behind]
        specs += [term, flat, flat]
    return call(
        functools.partial(mixer_result_kernel, wide),
        (rows // step,),
        specs,
        pl.BlockSpec((step, 4, local_width), lambda i, t: (i, 0, 0)),
        jax.ShapeDtypeStruct((rows, 4, local_width), F32),
        "mixer_result",
        table,
        *operands,
    )


def pack_kernel(wide, in_ref, out_ref):
    low = 0
    for group in range(in_ref.shape[2] // wide):
        for p in range(3):
            out_ref[:, low : low + wide] = in_ref[:, p, group * wide : (group + 1) * wide].astype(BF16)
            low += wide
    out_ref[:, low:] = in_ref[:, 3, :].astype(BF16)


def pack_mixer(weights, wide):
    rows, _, width = weights.shape
    step = 32
    return pl.pallas_call(
        functools.partial(pack_kernel, wide),
        grid=(rows // step,),
        in_specs=[pl.BlockSpec((step, 4, width), lambda i: (i, 0, 0))],
        out_specs=pl.BlockSpec((step, 4 * width), lambda i: (i, 0)),
        out_shape=jax.ShapeDtypeStruct((rows, 4 * width), BF16),
        cost_estimate=pl.CostEstimate(flops=1000, bytes_accessed=1000, transcendentals=0),
        name="pack_mixer",
    )(weights)


HEADS_PER_STEP = 2
PASSES = 3
PORTIONS = 4


class Box:
    def __init__(self, value):
        self.value = value


def sync(*boxes):
    values = lax.optimization_barrier(tuple(box.value for box in boxes))
    for box, value in zip(boxes, values):
        box.value = value


class Ring:
    def __init__(self, devices):
        self.chips = chips = devices // 2
        self.order = [2 * i for i in range(chips // 2)]
        self.order += [2 * i + 1 for i in reversed(range(chips // 2))]
        place = [self.order.index(c) for c in range(chips)]
        index = lax.axis_index("dp")
        chip, core = index // 2, index % 2
        here = jnp.asarray(place, jnp.int32)[chip]
        self.around = jnp.asarray(self.order, jnp.int32)[(here + jnp.arange(chips, dtype=jnp.int32)) % chips]
        self.cores = jnp.stack([core, 1 - core]).astype(jnp.int32)
        self.table = jnp.concatenate([2 * self.around + core, 2 * self.around + 1 - core])
        self.core_swap = [(i, i ^ 1) for i in range(devices)]
        self.hops = {}
        for turn in (1, -1):
            hops = []
            for at, source in enumerate(self.order):
                target = self.order[(at + turn) % chips]
                hops += [(2 * source, 2 * target), (2 * source + 1, 2 * target + 1)]
            self.hops[turn] = hops

    def send(self, value, turn):
        return Box(lax.ppermute(value, "dp", self.hops[turn]))

    def swap(self, value):
        return Box(lax.ppermute(value, "dp", self.core_swap))

    def steps(self, portion):
        total = self.chips // 2
        return range(total * portion // PORTIONS + 1, total * (portion + 1) // PORTIONS + 1)


class Gather:
    def __init__(self, ring, own):
        self.ring = ring
        box = Box(own)
        self.blocks = {(0, 0): [box]}
        self.front = {1: box, -1: box}
        self.fresh = [((0, 0), box)]
        self.pending = [box]

    def swap(self, boxes=None):
        if boxes is None:
            boxes, self.fresh = self.fresh, []
        for (at, _), box in boxes:
            other = self.ring.swap(box.value)
            self.blocks.setdefault((at, 1), []).append(other)
            self.pending.append(other)

    def advance(self, portion):
        chips = self.ring.chips
        came, self.fresh = self.fresh, []
        for step in self.ring.steps(portion):
            for turn in (1, -1):
                value = self.front[turn].value
                if 2 * step == chips:
                    half = value.shape[1] // 2
                    value = value[:, :half] if turn == 1 else value[:, half:]
                box = self.ring.send(value, turn)
                key = (-turn * step % chips, 0)
                self.blocks.setdefault(key, []).append(box)
                self.front[turn] = box
                self.fresh.append((key, box))
                self.pending.append(box)
        self.swap(came)

    def boxes(self):
        waiting, self.pending = self.pending, []
        return waiting

    def ordered(self):
        out = []
        for core in range(2):
            for at in range(self.ring.chips):
                parts = [box.value for box in self.blocks[at, core]]
                out.append(parts[0] if len(parts) == 1 else jnp.concatenate(parts, axis=1))
        return out


class Scatter:
    def __init__(self, ring, grads):
        self.ring = ring
        self.grads = grads
        self.other = Box(grads(1, None))
        self.own = None
        self.got = []

    def swap(self):
        self.other = self.ring.swap(self.other.value)

    def join(self):
        self.own = Box(self.grads(0, self.other.value))

    def advance(self, portion):
        chips = self.ring.chips
        for step in self.ring.steps(portion):
            away = chips // 2 - step + 1
            kind = {1: "first", 2: "second"}.get(step, "middle")
            got = [box.value for box in self.got]
            out = ring_hop(kind, self.own.value, got, self.ring.around, away, chips - away)
            self.got = [self.ring.send(out[0], 1), self.ring.send(out[1], -1)]

    def boxes(self):
        return [self.other if self.own is None else self.own] + self.got

    def parts(self):
        return [self.own.value, self.got[0].value, self.got[1].value]


class Exchange:
    def __init__(self, part, pieces):
        self.part = part
        blocks = part.shape[0] // 32
        self.cuts = [32 * (blocks * i // pieces) for i in range(pieces + 1)]
        self.got = []

    def advance(self):
        at = len(self.got)
        self.got.append(Box(swap_tensor(self.part[self.cuts[at] : self.cuts[at + 1]])))
        return self.got[-1]

    def result(self):
        other = jnp.concatenate([box.value for box in self.got], axis=0)
        return self.part.astype(F32) + other.astype(F32)


def swap_tensor(value):
    return lax.ppermute(value, "tensor", [(0, 1), (1, 0)])


def norm_back(values, scale, gain, grad):
    scaled = gain * grad
    inner = jnp.mean(values * scaled, axis=-1, keepdims=True)
    gain_grad = jnp.sum(values * scale * grad, axis=0)
    return scale * scaled - values * (scale * scale * scale) * inner, gain_grad


def matmul(left, right, dims):
    return lax.dot_general(left, right, dims, preferred_element_type=F32)


def even_blocks(matrix):
    return [matrix[i : i + 128] for i in range(0, matrix.shape[0], 128)]


def unit_chunks(units):
    tile = 256
    cut = units // tile * 3 // 4 * tile
    return [(0, cut), (cut, units)]


def body(
    tokens,
    segments,
    cotangent,
    norm_gain,
    attn_weight,
    beta_weight,
    conv_weight,
    out_gain,
    mlp_gain,
    mlp_weight,
):
    seg_ids = segments[0]
    length = tokens.shape[0]
    devices = lax.axis_size("dp")
    ring = Ring(devices)
    rows, _, local_width = attn_weight.shape
    head_count = beta_weight.shape[1]
    piece = conv_weight.shape[3]
    units = mlp_weight.shape[2]
    width = rows * devices
    groups = head_count // HEADS_PER_STEP
    wide = local_width // groups
    qkv = 3 * local_width
    taps_size = conv_weight.size
    chunks = unit_chunks(units)

    attn_local = pack_mixer(attn_weight, wide)
    small = jnp.concatenate(
        [norm_gain, mlp_gain, beta_weight.reshape(-1), conv_weight.reshape(-1), out_gain]
    ).astype(BF16)
    small = jnp.broadcast_to(small, (devices,) + small.shape)
    mlp_low = mlp_weight.astype(BF16)
    mlp_local = [
        Box(mlp_low[:, :, low:high].reshape(rows, 3 * (high - low))) for low, high in chunks
    ]

    in_ring = rows % 128 == 0
    if in_ring:
        attn = Gather(ring, attn_local)
        attn.advance(0)
    small = Box(lax.all_to_all(small, "dp", 0, 0, tiled=True))
    if in_ring:
        sync(*attn.boxes())
        attn.advance(1)
    at = [0, rows, 2 * rows, 2 * rows + rows * head_count]
    small = small.value
    gain_in = small[:, at[0] : at[1]].reshape(-1).astype(F32)
    gain_mid = small[:, at[1] : at[2]].reshape(-1).astype(F32)
    beta_mat = small[:, at[2] : at[3]].reshape(width, head_count)
    beta_pad = Box(jnp.pad(beta_mat, ((0, 0), (0, 128 - head_count))))
    taps = small[:, at[3] : at[3] + taps_size].reshape(devices, 3, 4, head_count, piece)
    taps = Box(taps.transpose(1, 2, 3, 0, 4).reshape(3, 4, local_width).astype(F32))
    gain_heads = Box(small[:, at[3] + taps_size :].reshape(1, -1).astype(F32))
    inputs_f = tokens.astype(F32)
    scale_in = lax.rsqrt(jnp.mean(inputs_f * inputs_f, axis=-1, keepdims=True) + 1e-05)
    normed = Box((inputs_f * scale_in * gain_in).astype(BF16))
    logits = Box(matmul(normed.value, beta_pad.value, NN))
    if in_ring:
        sync(*attn.boxes(), normed, logits, taps, gain_heads, beta_pad)
        attn.advance(2)
        sync(*attn.boxes(), normed, *mlp_local)
        attn.advance(3)
        sync(*attn.boxes(), normed, mlp_local[1])
        attn.swap()
        attn_blocks = attn.ordered()
        table = ring.table
    else:
        attn_blocks = even_blocks(lax.all_gather(attn_local, "dp", axis=0, tiled=True))
        table = jnp.arange(width // 128, dtype=jnp.int32)
    mats = [lax.all_gather(mlp_local[0].value, "dp", axis=0, tiled=True)]

    projected = Box(times_rows(normed.value, attn_blocks, table, 0, qkv, 512, F32))
    sync(projected, mlp_local[1])
    mats.append(lax.all_gather(mlp_local[1].value, "dp", axis=0, tiled=True))
    mixed, *saved = mixer_forward(
        projected.value,
        logits.value,
        taps.value,
        gain_heads.value,
        seg_ids,
        HEADS_PER_STEP,
        PASSES,
        0,
        groups,
    )
    part = times_turned([([mixed], attn_blocks, qkv)], table)
    hidden = inputs_f + part.astype(F32) + swap_tensor(part).astype(F32)
    scale_mid = lax.rsqrt(jnp.mean(hidden * hidden, axis=-1, keepdims=True) + 1e-05)
    normed_mlp = (hidden * scale_mid * gain_mid).astype(BF16)

    def mlp_grads(which):
        act = acts[which].value
        size = act.shape[2]
        pairs = [(normed_mlp, act, 0, 2), (cotangent, act, 2, 1)]
        tile = size // 2 if size % 512 == 0 else size

        def grads(half, plus):
            return weight_grads(pairs, tile, rows, ring.cores, half, plus)

        return grads

    acts = [Box(gated_units(normed_mlp, cotangent, mats[0], table, 256))]
    sync(*acts)
    sums = [Scatter(ring, mlp_grads(0))]
    sync(*acts, *sums[0].boxes())
    sums[0].swap()
    act = acts[0].value
    part = Box(units_turned([(act, p, mats[0]) for p in range(2)], 256, F32, table))
    sync(part, *acts, *sums[0].boxes())
    sums[0].join()
    sync(part, *acts, *sums[0].boxes())
    sums[0].advance(0)
    acts.append(Box(gated_units(normed_mlp, cotangent, mats[1], table, 256)))
    sync(part, *acts, *sums[0].boxes())
    sums[0].advance(1)
    act = acts[1].value
    part = Box(units_turned([(act, p, mats[1]) for p in range(2)], 256, BF16, table, plus=part.value))
    sync(part, *acts, *sums[0].boxes())
    exchange = Exchange(part.value, 3)
    sums[0].advance(2)
    sums.append(Scatter(ring, mlp_grads(1)))
    sync(exchange.advance(), *acts, *sums[0].boxes(), *sums[1].boxes())
    sums[0].advance(3)
    sums[1].swap()
    down = Box(units_turned([(a.value, 2, mat) for a, mat in zip(acts, mats)], 256, BF16, table))
    sync(exchange.advance(), down, *acts, *sums[0].boxes(), *sums[1].boxes())
    sums[1].join()
    sync(*sums[1].boxes())
    sums[1].advance(0)
    sync(exchange.advance(), *sums[1].boxes())
    sums[1].advance(1)

    grad_norm, grad_gain_mid = norm_back(hidden, scale_mid, gain_mid, exchange.result())
    grad_hidden = cotangent.astype(F32) + grad_norm
    grad_hidden_low = grad_hidden.astype(BF16)
    grad_mixed = Box(
        times_rows(grad_hidden_low, attn_blocks, table, qkv, local_width, 512, F32)
    )
    sync(*sums[1].boxes(), grad_mixed, down)
    sums[1].advance(2)
    down = Exchange(down.value, 3)

    def mixer_grads(first, count):
        made = mixer_backward(
            projected.value,
            logits.value,
            taps.value,
            gain_heads.value,
            seg_ids,
            saved,
            grad_mixed.value,
            HEADS_PER_STEP,
            PASSES,
            first,
            count,
            0,
        )
        return [Box(m) for m in made]

    half = groups // 2
    back = [mixer_grads(0, half)]
    sync(down.advance(), *sums[1].boxes(), back[0][0], grad_mixed)
    sums[1].advance(3)

    def early_grads(which, plus):
        pairs = [(normed.value, back[0][0].value, 0, 1), (grad_hidden_low, mixed, 0, 1)]
        return weight_grads(pairs, 512, rows, ring.cores, which, plus)

    first = Scatter(ring, early_grads)
    sync(*sums[1].boxes(), *first.boxes(), grad_mixed)
    first.swap()
    back.append(mixer_grads(half, half // 2))
    sync(down.advance(), back[1][0], grad_mixed, *first.boxes())
    first.join()
    sync(grad_mixed, *first.boxes())
    first.advance(0)
    back.append(mixer_grads(half + half // 2, half - half // 2))
    sync(down.advance(), back[2][0], *first.boxes())
    first.advance(1)
    grad_logits_low = sum(b[1].value for b in back).astype(BF16)
    lefts = [b[0].value for b in back]
    part = Box(times_turned([(lefts, attn_blocks, 0)], table, extra=(grad_logits_low, beta_pad.value)))
    sync(part, back[1][0], back[2][0], *first.boxes())
    exchange = Exchange(part.value, 3)
    first.advance(2)

    def late_grads(which, plus):
        pairs = [(normed.value, b[0].value, 0, 1) for b in back[1:]]
        return weight_grads(pairs, back[1][0].value.shape[1], rows, ring.cores, which, plus)

    second = Scatter(ring, late_grads)
    sync(exchange.advance(), back[1][0], back[2][0], *first.boxes(), *second.boxes())
    first.advance(3)
    second.swap()
    grad_beta = Box(matmul(normed.value, grad_logits_low, TN)[:, :head_count])
    mlp_grad = Box(units_result([s.parts() for s in sums], ring.around))
    sync(exchange.advance(), grad_beta, mlp_grad, *first.boxes(), *second.boxes())
    second.join()
    second.advance(0)
    result = Box((hidden + down.result()).astype(BF16))
    sync(exchange.advance(), result, *first.boxes(), *second.boxes())
    second.advance(1)
    grad_normed = exchange.result()
    grad_beta = grad_beta.value
    sync(*second.boxes())
    second.advance(2)
    sync(*second.boxes())
    second.advance(3)

    grad_first, grad_gain_in = norm_back(inputs_f, scale_in, gain_in, grad_normed)
    grad_inputs = grad_hidden + grad_first

    grad_gain_heads = sum(b[3].value[0] for b in back)
    grad_gain_heads = grad_gain_heads + swap_tensor(grad_gain_heads)
    grad_taps = jnp.concatenate([b[2].value for b in back], axis=2)
    grad_taps = grad_taps.reshape(3, 4, head_count, devices, piece).transpose(3, 0, 1, 2, 4)
    packed = jnp.concatenate(
        [
            grad_gain_in.reshape(devices, -1),
            grad_gain_mid.reshape(devices, -1),
            grad_beta.reshape(devices, -1),
            grad_taps.reshape(devices, -1),
            grad_gain_heads.reshape(devices, -1),
        ],
        axis=1,
    )
    packed = jnp.sum(lax.all_to_all(packed, "dp", 0, 0, tiled=True), axis=0)
    attn_grad = mixer_result([first.parts(), second.parts()], wide, local_width, ring.around)
    return (
        result.value,
        grad_inputs,
        packed[at[0] : at[1]],
        attn_grad,
        packed[at[2] : at[3]].reshape(rows, head_count),
        packed[at[3] : at[3] + taps_size].reshape(conv_weight.shape),
        packed[at[3] + taps_size :],
        packed[at[1] : at[2]],
        mlp_grad.value.transpose(1, 0, 2),
    )


def solution(mesh):
    return jax.shard_map(
        body,
        mesh=mesh,
        in_specs=(
            P("dp", None),
            P("dp", None),
            P("dp", None),
            P("dp"),
            P("dp", None, "tensor"),
            P("dp", "tensor"),
            P(None, None, "tensor", "dp"),
            P("dp"),
            P("dp"),
            P("dp", None, "tensor"),
        ),
        out_specs=(
            P("dp", None),
            P("dp", None),
            P("dp"),
            P("dp", None, "tensor"),
            P("dp", "tensor"),
            P(None, None, "tensor", "dp"),
            P("dp"),
            P("dp"),
            P("dp", None, "tensor"),
        ),
        check_vma=False,
    )
```

```python
import functools

import jax
import jax.numpy as jnp
from jax import lax
from jax.experimental import pallas as pl
from jax.experimental.pallas import tpu as pltpu
from jax.sharding import PartitionSpec as P

F32 = jnp.float32
BF16 = jnp.bfloat16
CHUNK = 128
NN = (((1,), (0,)), ((), ()))
NT = (((1,), (1,)), ((), ()))
TN = (((0,), (0,)), ((), ()))


def split2(value):
    high = value.astype(BF16)
    return high, (value - high.astype(F32)).astype(BF16)


def dot1(left, right, dims):
    return lax.dot_general(left, right, dims, preferred_element_type=F32)


def mul3(left, right, dims):
    (lh, ll), (rh, rl) = left, right
    return dot1(lh, rh, dims) + (dot1(lh, rl, dims) + dot1(ll, rh, dims))


def mul1(left, right, dims):
    return dot1(left[0], right[0], dims)


def iotas(size):
    return (
        lax.broadcasted_iota(jnp.int32, (size, size), 0),
        lax.broadcasted_iota(jnp.int32, (size, size), 1),
    )


def allowed_rows(seg_full, offset):
    rows = lax.broadcasted_iota(jnp.int32, seg_full.shape, 0)
    earlier = pltpu.roll(seg_full, offset, 0)
    return jnp.where((earlier == seg_full) & (rows >= offset), 1.0, 0.0).astype(F32)


def conv_taps(signal, taps, gates):
    summed = signal * taps[3:4]
    for offset in range(1, 4):
        summed = summed + pltpu.roll(signal, offset, 0) * gates[offset - 1] * taps[3 - offset : 4 - offset]
    return summed


def chunk_masks(segc_ref, segr_ref, chunk):
    start = chunk * CHUNK
    col = segc_ref[start : start + CHUNK, :]
    row = segr_ref[:, start : start + CHUNK]
    same = col == row
    last = segc_ref[start + CHUNK - 1 : start + CHUNK, :]
    if chunk == 0:
        carry = jnp.zeros(col.shape, F32)
        carry_last = jnp.zeros(last.shape, F32)
    else:
        prior = segc_ref[start - 1 : start, :]
        carry = (col == prior).astype(F32)
        carry_last = (last == prior).astype(F32)
    tail = (col == last).astype(F32)
    return same, carry, carry_last, tail


def head_logits(beta_ref, head):
    lanes = lax.broadcasted_iota(jnp.int32, beta_ref.shape, 1)
    return jnp.sum(jnp.where(lanes == head, beta_ref[...], 0.0), axis=1, keepdims=True)


def forward_kernel(heads, passes, first, proj_ref, beta_ref, conv_ref, gain_ref, segc_ref, segr_ref,
                   mixed_ref, out_ref, writes_ref, solve_ref, state_ref, q_scr, k_scr, v_scr):
    group = first + pl.program_id(0)
    length = proj_ref.shape[0]
    chunks = length // CHUNK
    width = 128
    mul = mul3 if passes == 3 else mul1
    seg_full = jnp.broadcast_to(segc_ref[...], (length, width))
    gates = [allowed_rows(seg_full, offset) for offset in (1, 2, 3)]
    betas = []
    for h in range(heads):
        for which, scr in enumerate((q_scr, k_scr, v_scr)):
            column = (which * heads + h) * width
            signal = proj_ref[:, column : column + width]
            mixed_in = conv_taps(signal, conv_ref[which, :, h * width : (h + 1) * width], gates)
            value = mixed_in * jax.nn.sigmoid(mixed_in)
            if which < 2:
                value = value * lax.rsqrt(jnp.sum(value * value, axis=1, keepdims=True) + 1e-6)
            scr[:, h * width : (h + 1) * width] = value
        betas.append(jax.nn.sigmoid(head_logits(beta_ref, group * heads + h)))
    rows, cols = iotas(CHUNK)
    masks = [chunk_masks(segc_ref, segr_ref, c) for c in range(chunks)]
    items = [(h, c) for c in range(chunks) for h in range(heads)]

    def part(scr, h, c):
        return scr[c * CHUNK : (c + 1) * CHUNK, h * width : (h + 1) * width]

    def beta_of(h, c):
        return betas[h][c * CHUNK : (c + 1) * CHUNK]

    system, inverse = {}, {}
    for h, c in items:
        keys = split2(part(k_scr, h, c))
        inner = mul(keys, keys, NT)
        keep = masks[c][0] & (rows > cols)
        system[h, c] = jnp.where(keep, inner * beta_of(h, c), 0.0)
        first = (rows // 2 == cols // 2)
        inverse[h, c] = jnp.where(rows == cols, 1.0, jnp.where(first, -system[h, c], 0.0))
    size = 2
    while size < CHUNK:
        off = (rows // (2 * size) == cols // (2 * size)) & (rows // size != cols // size)
        mid = {}
        for it in items:
            step = jnp.where(off, system[it], 0.0)
            if passes == 3:
                mid[it] = mul3(split2(inverse[it]), split2(step), NN)
            else:
                mid[it] = dot1(inverse[it].astype(BF16), step.astype(BF16), NN)
        for it in items:
            if passes == 3:
                inverse[it] = inverse[it] - mul3(split2(mid[it]), split2(inverse[it]), NN)
            else:
                inverse[it] = inverse[it] - dot1(mid[it].astype(BF16), inverse[it].astype(BF16), NN)
        size *= 2
    scores, fresh, decay = {}, {}, {}
    for h, c in items:
        same, carry, carry_last, tail = masks[c]
        keys, queries, values = part(k_scr, h, c), part(q_scr, h, c), part(v_scr, h, c)
        scores[h, c] = split2(jnp.where(same & (rows >= cols), mul(split2(queries), split2(keys), NT), 0.0))
        solver = split2(inverse[h, c])
        fresh[h, c] = mul(solver, split2(values * beta_of(h, c)), NN)
        decay[h, c] = split2(mul(solver, split2(keys * (beta_of(h, c) * carry)), NN))
        solve_ref[c * CHUNK : (c + 1) * CHUNK, h * width : (h + 1) * width] = inverse[h, c]
    state = {h: jnp.zeros((width, width), F32) for h in range(heads)}
    gain = gain_ref[...]
    for c in range(chunks):
        same, carry, carry_last, tail = masks[c]
        span = slice(c * CHUNK, (c + 1) * CHUNK)
        for h in range(heads):
            state_ref[span, h * width : (h + 1) * width] = state[h]
        writes = {}
        if c == 0:
            for h in range(heads):
                writes[h] = fresh[h, c]
        else:
            split_state = {h: split2(state[h]) for h in range(heads)}
            for h in range(heads):
                writes[h] = fresh[h, c] - mul(decay[h, c], split_state[h], NN)
        for h in range(heads):
            lanes = slice(h * width, (h + 1) * width)
            writes_ref[span, lanes] = writes[h]
            result = mul(scores[h, c], split2(writes[h]), NN)
            if c > 0:
                result = result + carry * mul(split2(part(q_scr, h, c)), split_state[h], NN)
            out_ref[span, lanes] = result
            scale = lax.rsqrt(jnp.mean(result * result, axis=1, keepdims=True) + 1e-5)
            mixed_ref[span, lanes] = (result * scale * gain).astype(BF16)
        if c + 1 < chunks:
            for h in range(heads):
                add = mul(split2(part(k_scr, h, c)), split2(writes[h] * tail), TN)
                state[h] = carry_last * state[h] + add


def backward_kernel(heads, passes, first, proj_ref, beta_ref, conv_ref, gain_ref, segc_ref, segr_ref,
                    out_ref, writes_ref, solve_ref, state_ref, gmix_ref,
                    gproj_ref, gbeta_ref, gconv_ref, ggain_ref,
                    q_scr, k_scr, v_scr, gq_scr, gk_scr, gv_scr, do_scr):
    group = first + pl.program_id(0)
    length = proj_ref.shape[0]
    chunks = length // CHUNK
    width = 128
    mul = mul3 if passes == 3 else mul1
    seg_full = jnp.broadcast_to(segc_ref[...], (length, width))
    gates = [allowed_rows(seg_full, offset) for offset in (1, 2, 3)]
    gain = gain_ref[...]

    @pl.when(pl.program_id(0) == 0)
    def _():
        gbeta_ref[...] = jnp.zeros_like(gbeta_ref)
        ggain_ref[...] = jnp.zeros_like(ggain_ref)

    def convolved(which, h):
        column = (which * heads + h) * width
        signal = proj_ref[:, column : column + width]
        mixed_in = conv_taps(signal, conv_ref[which, :, h * width : (h + 1) * width], gates)
        gate = jax.nn.sigmoid(mixed_in)
        return signal, mixed_in, gate

    betas = []
    for h in range(heads):
        lanes = slice(h * width, (h + 1) * width)
        for which, scr in enumerate((q_scr, k_scr, v_scr)):
            _, mixed_in, gate = convolved(which, h)
            value = mixed_in * gate
            if which < 2:
                value = value * lax.rsqrt(jnp.sum(value * value, axis=1, keepdims=True) + 1e-6)
            scr[:, lanes] = value
        betas.append(jax.nn.sigmoid(head_logits(beta_ref, group * heads + h)))
        result, grad = out_ref[:, lanes], gmix_ref[:, lanes]
        scale = lax.rsqrt(jnp.mean(result * result, axis=1, keepdims=True) + 1e-5)
        unit = result * scale
        ggain_ref[...] += jnp.sum(unit * grad, axis=0, keepdims=True)
        scaled = grad * gain
        do_scr[:, lanes] = scale * (scaled - unit * jnp.mean(unit * scaled, axis=1, keepdims=True))
    rows, cols = iotas(CHUNK)
    masks = [chunk_masks(segc_ref, segr_ref, c) for c in range(chunks)]
    items = [(h, c) for c in range(chunks) for h in range(heads)]

    def part(scr, h, c):
        return scr[c * CHUNK : (c + 1) * CHUNK, h * width : (h + 1) * width]

    def beta_of(h, c):
        return betas[h][c * CHUNK : (c + 1) * CHUNK]

    inner, base, reach, gscore = {}, {}, {}, {}
    for h, c in items:
        same, carry, carry_last, tail = masks[c]
        keys, queries = split2(part(k_scr, h, c)), split2(part(q_scr, h, c))
        grads, writes = split2(part(do_scr, h, c)), split2(part(writes_ref, h, c))
        inner[h, c] = mul(keys, keys, NT)
        causal = same & (rows >= cols)
        scores = split2(jnp.where(causal, mul(queries, keys, NT), 0.0))
        solver = split2(part(solve_ref, h, c))
        base[h, c] = mul(solver, split2(mul(scores, grads, TN)), TN)
        if c + 1 < chunks:
            reach[h, c] = split2(mul(solver, split2(part(k_scr, h, c) * tail), TN))
        gscore = split2(jnp.where(causal, mul(grads, writes, NT), 0.0))
        gq = mul(gscore, keys, NN)
        gk = mul(gscore, queries, TN)
        span, lanes = slice(c * CHUNK, (c + 1) * CHUNK), slice(h * width, (h + 1) * width)
        if c > 0:
            gq = gq + mul(split2(part(do_scr, h, c) * carry), split2(part(state_ref, h, c)), NT)
        gq_scr[span, lanes] = gq
        gk_scr[span, lanes] = gk
    gstate = {}
    gbetas = {}
    for c in reversed(range(chunks)):
        same, carry, carry_last, tail = masks[c]
        span = slice(c * CHUNK, (c + 1) * CHUNK)
        gtarget = {}
        for h in range(heads):
            gtarget[h] = base[h, c]
            if c + 1 < chunks:
                gtarget[h] = gtarget[h] + mul(reach[h, c], split2(gstate[h]), NN)
        for h in range(heads):
            lanes = slice(h * width, (h + 1) * width)
            gk = gk_scr[span, lanes]
            keys = split2(part(k_scr, h, c))
            beta = beta_of(h, c)
            writes = part(writes_ref, h, c)
            split_target = split2(gtarget[h])
            if c + 1 < chunks:
                gk = gk + mul(split2(writes * tail), split2(gstate[h]), NT)
            strict = same & (rows > cols)
            gsys = jnp.where(strict, mul(split_target, split2(writes), NT), 0.0)
            ginner = split2(gsys * beta)
            gbeta = -jnp.sum(gsys * inner[h, c], axis=1, keepdims=True)
            gk = gk - mul(ginner, keys, NN) - mul(ginner, keys, TN)
            target = part(v_scr, h, c)
            if c > 0:
                states = split2(part(state_ref, h, c))
                target = target - carry * mul(keys, states, NN)
                grecall = gtarget[h] * (beta * carry)
                split_recall = split2(grecall)
                gk = gk - mul(split_recall, states, NT)
                new_state = mul(split2(part(q_scr, h, c)), split2(part(do_scr, h, c) * carry), TN)
                new_state = new_state - mul(keys, split_recall, TN)
                if c + 1 < chunks:
                    new_state = new_state + carry_last * gstate[h]
                gstate[h] = new_state
            gbeta = gbeta + jnp.sum(gtarget[h] * target, axis=1, keepdims=True)
            gbetas[h, c] = gbeta * beta * (1.0 - beta)
            gk_scr[span, lanes] = gk
            gv_scr[span, lanes] = gtarget[h] * beta
    for c in range(chunks):
        span = slice(c * CHUNK, (c + 1) * CHUNK)
        lane_ids = lax.broadcasted_iota(jnp.int32, (CHUNK, gbeta_ref.shape[1]), 1)
        total = gbeta_ref[span, :]
        for h in range(heads):
            total = jnp.where(lane_ids == group * heads + h, gbetas[h, c], total)
        gbeta_ref[span, :] = total
    for h in range(heads):
        lanes = slice(h * width, (h + 1) * width)
        for which, (scr, gscr) in enumerate(((q_scr, gq_scr), (k_scr, gk_scr), (v_scr, gv_scr))):
            signal, mixed_in, gate = convolved(which, h)
            grad = gscr[:, lanes]
            if which < 2:
                value = mixed_in * gate
                scale = lax.rsqrt(jnp.sum(value * value, axis=1, keepdims=True) + 1e-6)
                unit = value * scale
                grad = scale * (grad - unit * jnp.sum(unit * grad, axis=1, keepdims=True))
            grad = grad * gate * (1.0 + mixed_in * (1.0 - gate))
            taps = conv_ref[which, :, h * width : (h + 1) * width]
            gsignal = grad * taps[3:4]
            gtaps = [None] * 4
            gtaps[3] = jnp.sum(grad * signal, axis=0, keepdims=True)
            for offset in range(1, 4):
                gated = grad * gates[offset - 1]
                gtaps[3 - offset] = jnp.sum(gated * pltpu.roll(signal, offset, 0), axis=0, keepdims=True)
                gsignal = gsignal + pltpu.roll(gated, length - offset, 0) * taps[3 - offset : 4 - offset]
            gconv_ref[which, :, lanes] = jnp.concatenate(gtaps, axis=0)
            column = (which * heads + h) * width
            gproj_ref[:, column : column + width] = gsignal.astype(BF16)


def mixer_specs(length, wide, first, skip):
    fixed = lambda shape: pl.BlockSpec(shape, lambda g: (0,) * len(shape))
    return [
        pl.BlockSpec((length, 3 * wide), lambda g: (0, g + skip)),
        fixed((length, 128)),
        pl.BlockSpec((3, 4, wide), lambda g: (0, 0, g + first)),
        fixed((1, 128)),
        fixed((length, 1)),
        fixed((1, length)),
    ]


CHEAP = pl.CostEstimate(flops=1000, bytes_accessed=1000, transcendentals=0)


def mixer_forward(projected, logits, conv, gain, seg_ids, heads, passes, first):
    length = projected.shape[0]
    wide = heads * 128
    count = projected.shape[1] // (3 * wide)
    f32 = jax.ShapeDtypeStruct((length, count * wide), F32)
    block = pl.BlockSpec((length, wide), lambda g: (0, g))
    return pl.pallas_call(
        functools.partial(forward_kernel, heads, passes, first),
        grid=(count,),
        in_specs=mixer_specs(length, wide, first, 0),
        out_specs=[block] * 5,
        out_shape=[jax.ShapeDtypeStruct((length, count * wide), BF16), f32, f32, f32, f32],
        scratch_shapes=[pltpu.VMEM((length, wide), F32)] * 3,
        compiler_params=pltpu.CompilerParams(vmem_limit_bytes=60 * 2**20),
        cost_estimate=CHEAP,
        name="mixer_forward",
    )(projected, logits, conv, gain, seg_ids[:, None], seg_ids[None, :])


def mixer_backward(projected, logits, conv, gain, seg_ids, saved, grad_mixed, heads, passes, first, skip):
    length = projected.shape[0]
    wide = heads * 128
    block = pl.BlockSpec((length, wide), lambda g: (0, g + skip))
    grads = pl.BlockSpec((length, wide), lambda g: (0, g + first))
    fixed = lambda shape: pl.BlockSpec(shape, lambda g: (0,) * len(shape))
    outs = [
        jax.ShapeDtypeStruct((length, 3 * wide), BF16),
        jax.ShapeDtypeStruct((length, 128), F32),
        jax.ShapeDtypeStruct((3, 4, wide), F32),
        jax.ShapeDtypeStruct((1, 128), F32),
    ]
    return pl.pallas_call(
        functools.partial(backward_kernel, heads, passes, first),
        grid=(1,),
        in_specs=mixer_specs(length, wide, first, skip) + [block] * 4 + [grads],
        out_specs=[fixed(out.shape) for out in outs],
        out_shape=outs,
        scratch_shapes=[pltpu.VMEM((length, wide), F32)] * 7,
        compiler_params=pltpu.CompilerParams(vmem_limit_bytes=50 * 2**20),
        cost_estimate=CHEAP,
        name="mixer_backward",
    )(projected, logits, conv, gain, seg_ids[:, None], seg_ids[None, :], *saved, grad_mixed)


def whole(array):
    return pl.BlockSpec(array.shape, lambda *_: (0,) * array.ndim)


def room(name):
    return (40 if name == "weight_grads" else 50) * 2**20


def call(kernel, grid, in_specs, out_specs, out_shape, name, table, *operands, scratch=()):
    return pl.pallas_call(
        kernel,
        grid_spec=pltpu.PrefetchScalarGridSpec(
            num_scalar_prefetch=1,
            grid=grid,
            in_specs=in_specs,
            out_specs=out_specs,
            scratch_shapes=scratch,
        ),
        out_shape=out_shape,
        compiler_params=pltpu.CompilerParams(vmem_limit_bytes=room(name)),
        cost_estimate=CHEAP,
        name=name,
    )(table, *operands)


IN_PLACE = pl.BlockSpec(memory_space=pl.ANY)


def lanes_at(place, width):
    return pl.ds(pl.multiple_of(place * width, width), width)


def column_tiles(blocks, starts, tile, table_ref, hold, sems):
    rows = blocks[0].shape[0]
    step, count = pl.program_id(0), pl.num_programs(0)

    def copies(at):
        slot = lax.rem(at, 2)
        for w, start in enumerate(starts):
            columns = pl.ds(pl.multiple_of(start + at * tile, 128), tile)
            for r, block in enumerate(blocks):
                yield pltpu.make_async_copy(
                    block.at[:, columns],
                    hold.at[slot, w, lanes_at(table_ref[r], rows), :],
                    sems.at[slot, w, r],
                )

    @pl.when(step == 0)
    def _():
        for copy in copies(step):
            copy.start()

    @pl.when(step + 1 < count)
    def _():
        for copy in copies(step + 1):
            copy.start()

    for copy in copies(step):
        copy.wait()
    return lax.rem(step, 2)


def tile_scratch(blocks, ranges, tile):
    rows, count = blocks[0].shape[0], len(blocks)
    return [
        pltpu.VMEM((2, ranges, rows * count, tile), BF16),
        pltpu.SemaphoreType.DMA((2, ranges, count)),
    ]


def rows_kernel(count, start, tile, table_ref, left_ref, *refs):
    blocks, (out_ref, hold, sems) = refs[:count], refs[count:]
    slot = column_tiles(blocks, [start], tile, table_ref, hold, sems)
    out_ref[...] = dot1(left_ref[...], hold[slot, 0], NN).astype(out_ref.dtype)


def times_rows(left, blocks, table, start, columns, tile, kind):
    return call(
        functools.partial(rows_kernel, len(blocks), start, tile),
        (columns // tile,),
        [whole(left)] + [IN_PLACE] * len(blocks),
        pl.BlockSpec((left.shape[0], tile), lambda i, t: (0, i)),
        jax.ShapeDtypeStruct((left.shape[0], columns), kind),
        "times_rows",
        table,
        left,
        *blocks,
        scratch=tile_scratch(blocks, 1, tile),
    )


def gated_kernel(table_ref, normed_ref, cot_ref, gate_ref, up_ref, down_ref, out_ref):
    gate = dot1(normed_ref[...], gate_ref[...], NN)
    up = dot1(normed_ref[...], up_ref[...], NN)
    grad = dot1(cot_ref[...], down_ref[...], NN)
    sig = jax.nn.sigmoid(gate)
    silu = gate * sig
    out_ref[0] = (grad * up * sig * (1.0 + gate * (1.0 - sig))).astype(BF16)
    out_ref[1] = (grad * silu).astype(BF16)
    out_ref[2] = (silu * up).astype(BF16)


def gated_units(normed, cot, mat, table, tile):
    width, columns = mat.shape
    units = columns // 3
    each = units // tile
    length = normed.shape[0]

    def spec(which):
        return pl.BlockSpec((width, tile), lambda i, t: (0, which * each + i))

    return call(
        gated_kernel,
        (each,),
        [whole(normed), whole(cot)] + [spec(w) for w in range(3)],
        pl.BlockSpec((3, length, tile), lambda i, t: (0, 0, i)),
        jax.ShapeDtypeStruct((3, length, units), BF16),
        "gated_units",
        table,
        normed,
        cot,
        mat,
        mat,
        mat,
    )


def units_kernel(terms, plus, table_ref, *refs):
    out_ref = refs[-1]
    total = refs[2 * terms][...] if plus else None
    for n in range(terms):
        part = dot1(refs[n][...], refs[terms + n][...], NT)
        total = part if total is None else total + part
    out_ref[...] = total.astype(out_ref.dtype)


def units_turned(terms, tile, kind, table, plus=None):
    acts, mats, act_specs, mat_specs = [], [], [], []
    for act, plane, mat in terms:
        length, units = act.shape[1:]
        width = mat.shape[0]
        acts.append(act)
        mats.append(mat)
        act_specs.append(pl.BlockSpec((None, length, units), lambda i, t, p=plane: (p, 0, 0)))
        mat_specs.append(pl.BlockSpec((tile, units), lambda i, t, p=plane: (i, p)))
    column = pl.BlockSpec((length, tile), lambda i, t: (0, i))
    more = [] if plus is None else [plus]
    return call(
        functools.partial(units_kernel, len(terms), len(more)),
        (width // tile,),
        act_specs + mat_specs + [column for _ in more],
        column,
        jax.ShapeDtypeStruct((length, width), kind),
        "units_turned",
        table,
        *acts,
        *mats,
        *more,
    )


def turned_kernel(plan, extra, table_ref, *refs):
    lefts = refs[: sum(len(pieces) for _, _, _, pieces in plan)]
    refs = refs[len(lefts) :]
    blocks = []
    for count, _, _, _ in plan:
        blocks.append(refs[:count])
        refs = refs[count:]
    tail, refs = refs[:extra], refs[extra:]
    out_ref, sems, holds = refs[0], refs[1], refs[2:]
    step, last = pl.program_id(0), pl.num_programs(0) - 1
    rows = blocks[0][0].shape[0]
    count = len(blocks[0])

    def copies(r):
        for g, (_, start, width, _) in enumerate(plan):
            yield pltpu.make_async_copy(
                blocks[g][r].at[:, start : start + width],
                holds[g].at[r // 2 % 2, r % 2 * rows : (r % 2 + 1) * rows, :],
                sems.at[g, r // 2 % 2, r % 2],
            )

    for r in range(count):
        if r < 2:

            @pl.when(step == 0)
            def _():
                for copy in copies(r):
                    copy.start()

        else:

            @pl.when(step + 1 == r // 2)
            def _():
                for copy in copies(r):
                    copy.start()

    for r in range(count):

        @pl.when(step == r // 2)
        def _():
            for copy in copies(r):
                copy.wait()

    slot = lax.rem(step, 2)
    total, at = None, 0
    for g, (_, _, _, pieces) in enumerate(plan):
        low = 0
        for plane in pieces:
            left = lefts[at][plane] if plane is not None else lefts[at][...]
            high = low + left.shape[1]
            part = dot1(left, holds[g][slot, :, low:high], NT)
            total = part if total is None else total + part
            low, at = high, at + 1
    for k in range(2):
        place = table_ref[2 * step + k]
        piece = total[:, k * rows : (k + 1) * rows]
        if extra:
            piece = piece + dot1(tail[0][...], tail[1][lanes_at(place, rows), :], NT)
        out_ref[:, lanes_at(place, rows)] = piece.astype(BF16)


def times_turned(groups, table, extra=()):
    plan, lefts, left_specs, blocks = [], [], [], []
    for pieces, own_blocks, start in groups:
        width, planes = 0, []
        for piece in pieces:
            if isinstance(piece, tuple):
                piece, plane = piece
                planes.append(0)
                left_specs.append(
                    pl.BlockSpec((1,) + piece.shape[1:], lambda i, t, plane=plane: (plane, 0, 0))
                )
            else:
                planes.append(None)
                left_specs.append(whole(piece))
            lefts.append(piece)
            width += piece.shape[-1]
        plan.append((len(own_blocks), start, width, planes))
        blocks += own_blocks
    rows, count = groups[0][1][0].shape[0], plan[0][0]
    length = lefts[0].shape[-2]
    out = jax.ShapeDtypeStruct((length, rows * count), BF16)
    return call(
        functools.partial(turned_kernel, plan, len(extra)),
        (count // 2,),
        left_specs + [IN_PLACE] * len(blocks) + [whole(a) for a in extra],
        whole(out),
        out,
        "times_turned",
        table,
        *lefts,
        *blocks,
        *extra,
        scratch=[pltpu.SemaphoreType.DMA((len(plan), 2, 2))]
        + [pltpu.VMEM((2, 2 * rows, width), BF16) for _, _, width, _ in plan],
    )


def weight_kernel(cuts, which, plus, table_ref, *refs):
    pairs = len(cuts) - 1
    lefts, rights, out_ref, turned = refs[:pairs], refs[pairs : 2 * pairs], refs[-2], refs[-1]
    step = pl.program_id(0)
    block = 128
    for n in range(pairs):

        @pl.when(step == cuts[n])
        def _():
            for at in range(turned.shape[0] // block):
                if which is None:
                    lanes = slice(at * block, (at + 1) * block)
                else:
                    lanes = lanes_at(2 * at + table_ref[which], block)
                turned[at * block : (at + 1) * block, :] = lefts[n][:, lanes].T

        @pl.when((step >= cuts[n]) & (step < cuts[n + 1]))
        def _():
            product = dot1(turned[...], rights[n][...], NN)
            if plus:
                product = product + refs[2 * pairs][...].reshape(product.shape).astype(F32)
            out_ref[...] = product.astype(BF16).reshape(out_ref.shape)


def weight_grads(pairs, tile, rows, cores, which, plus=None):
    length, features = pairs[0][0].shape
    chips = features // (2 * rows)
    inside = rows % 128 == 0
    cuts, lefts, rights, specs = [0], [], [], []
    for left, right, plane, planes in pairs:
        if not inside:
            left = left.reshape(length, chips, 2, rows)
            left = lax.dynamic_index_in_dim(left, cores[which], 2, keepdims=False)
            left = left.reshape(length, chips * rows)
        each = right.shape[-1] // tile
        low, most = cuts[-1], planes * each - 1
        if right.ndim == 3:
            spec = pl.BlockSpec(
                (None, length, tile),
                lambda i, t, low=low, most=most, plane=plane, each=each: (
                    plane + jnp.clip(i - low, 0, most) // each,
                    0,
                    jnp.clip(i - low, 0, most) % each,
                ),
            )
        else:
            spec = pl.BlockSpec(
                (length, tile), lambda i, t, low=low, most=most: (0, jnp.clip(i - low, 0, most))
            )
        lefts.append(left)
        rights.append(right)
        specs.append(spec)
        cuts.append(low + most + 1)
    place = pl.BlockSpec((chips, rows, tile), lambda i, t: (0, 0, i))
    more = [] if plus is None else [plus]
    return call(
        functools.partial(weight_kernel, cuts, which if inside else None, len(more)),
        (cuts[-1],),
        [whole(left) for left in lefts] + specs + [place for _ in more],
        place,
        jax.ShapeDtypeStruct((chips, rows, cuts[-1] * tile), BF16),
        "weight_grads",
        cores,
        *lefts,
        *rights,
        *more,
        scratch=[pltpu.VMEM((chips * rows, length), BF16)],
    )


def hop_tile(half):
    for parts in (2, 3, 1):
        if half % (128 * parts) == 0:
            return half // parts
    return 128


def hop_kernel(kind, each, table_ref, *refs):
    step = pl.program_id(0)
    for d in range(2):
        total = refs[d][...]
        if kind == "first":
            refs[2 + d][...] = total
        elif kind == "middle":
            refs[4 + d][...] = (total.astype(F32) + refs[2 + d][...].astype(F32)).astype(BF16)
        else:
            mine = (step < each) if d == 0 else (step >= each)

            @pl.when(mine)
            def _():
                refs[4 + d][...] = (total.astype(F32) + refs[2 + d][...].astype(F32)).astype(BF16)

            @pl.when(jnp.logical_not(mine))
            def _():
                refs[4 + d][...] = total


def ring_hop(kind, own, got, table, ahead, behind):
    chips, rows, columns = own.shape
    half = columns // 2
    tile = hop_tile(half)
    each = half // tile

    def term(place, offset=0):
        return pl.BlockSpec((None, rows, tile), lambda i, t: (t[place], 0, i + offset))

    flat = pl.BlockSpec((rows, tile), lambda i, t: (0, i))
    if kind == "first":
        specs = [term(ahead), term(behind, each)]
        steps, width = each, half
    else:
        specs = [term(ahead), term(behind)]
        steps, width = 2 * each, columns
        if kind == "middle":
            specs += [flat, flat]
        else:
            specs += [
                pl.BlockSpec((rows, tile), lambda i, t: (0, jnp.minimum(i, each - 1))),
                pl.BlockSpec((rows, tile), lambda i, t: (0, jnp.maximum(i - each, 0))),
            ]
    return call(
        functools.partial(hop_kernel, kind, each),
        (steps,),
        specs,
        [flat, flat],
        [jax.ShapeDtypeStruct((rows, width), BF16)] * 2,
        "ring_hop",
        table,
        own,
        own,
        *got,
    )


def landed(refs):
    return refs[0][...].astype(F32) + refs[1][...].astype(F32) + refs[2][...].astype(F32)


def units_result_kernel(table_ref, *refs):
    low = 0
    for n in range(0, len(refs) - 1, 3):
        total = landed(refs[n : n + 3])
        refs[-1][:, low : low + total.shape[1]] = total
        low += total.shape[1]


def units_result(sums, table):
    operands, specs, units = [], [], 0
    for own, ahead, behind in sums:
        _, rows, columns = own.shape
        units += columns // 3
        term = pl.BlockSpec((None, rows, columns // 3), lambda i, t: (t[0], 0, i))
        flat = pl.BlockSpec((rows, columns // 3), lambda i, t: (0, i))
        operands += [own, ahead, behind]
        specs += [term, flat, flat]
    return call(
        units_result_kernel,
        (3,),
        specs,
        pl.BlockSpec((None, rows, units), lambda i, t: (i, 0, 0)),
        jax.ShapeDtypeStruct((3, rows, units), F32),
        "units_result",
        table,
        *operands,
    )


def mixer_result_kernel(wide, table_ref, *refs):
    out_ref = refs[-1]
    group = 0
    for n in range(0, len(refs) - 1, 3):
        total = landed(refs[n : n + 3])
        columns = total.shape[1]
        low = 0
        while columns - low >= 3 * wide and (n > 0 or columns - low > out_ref.shape[2]):
            for p in range(3):
                out_ref[:, p, group * wide : (group + 1) * wide] = total[:, low : low + wide]
                low += wide
            group += 1
        if low < columns:
            out_ref[:, 3, :] = total[:, low:]


def mixer_result(sums, wide, local_width, table):
    operands, specs = [], []
    step = 32
    for own, ahead, behind in sums:
        _, rows, columns = own.shape
        term = pl.BlockSpec((None, step, columns), lambda i, t: (t[0], i, 0))
        flat = pl.BlockSpec((step, columns), lambda i, t: (i, 0))
        operands += [own, ahead, behind]
        specs += [term, flat, flat]
    return call(
        functools.partial(mixer_result_kernel, wide),
        (rows // step,),
        specs,
        pl.BlockSpec((step, 4, local_width), lambda i, t: (i, 0, 0)),
        jax.ShapeDtypeStruct((rows, 4, local_width), F32),
        "mixer_result",
        table,
        *operands,
    )


def pack_kernel(wide, in_ref, out_ref):
    low = 0
    for group in range(in_ref.shape[2] // wide):
        for p in range(3):
            out_ref[:, low : low + wide] = in_ref[:, p, group * wide : (group + 1) * wide].astype(BF16)
            low += wide
    out_ref[:, low:] = in_ref[:, 3, :].astype(BF16)


def pack_mixer(weights, wide):
    rows, _, width = weights.shape
    step = 32
    return pl.pallas_call(
        functools.partial(pack_kernel, wide),
        grid=(rows // step,),
        in_specs=[pl.BlockSpec((step, 4, width), lambda i: (i, 0, 0))],
        out_specs=pl.BlockSpec((step, 4 * width), lambda i: (i, 0)),
        out_shape=jax.ShapeDtypeStruct((rows, 4 * width), BF16),
        cost_estimate=CHEAP,
        name="pack_mixer",
    )(weights)


HEADS_PER_STEP = 2
PASSES = 3
PORTIONS = 4


class Box:
    def __init__(self, value):
        self.value = value


def sync(*boxes):
    values = lax.optimization_barrier(tuple(box.value for box in boxes))
    for box, value in zip(boxes, values):
        box.value = value


class Ring:
    def __init__(self, devices):
        self.chips = chips = devices // 2
        self.order = [2 * i for i in range(chips // 2)]
        self.order += [2 * i + 1 for i in reversed(range(chips // 2))]
        place = [self.order.index(c) for c in range(chips)]
        index = lax.axis_index("dp")
        chip, core = index // 2, index % 2
        here = jnp.asarray(place, jnp.int32)[chip]
        self.around = jnp.asarray(self.order, jnp.int32)[(here + jnp.arange(chips, dtype=jnp.int32)) % chips]
        self.cores = jnp.stack([core, 1 - core]).astype(jnp.int32)
        self.table = jnp.concatenate([2 * self.around + core, 2 * self.around + 1 - core])
        self.core_swap = [(i, i ^ 1) for i in range(devices)]
        self.hops = {}
        for turn in (1, -1):
            hops = []
            for at, source in enumerate(self.order):
                target = self.order[(at + turn) % chips]
                hops += [(2 * source, 2 * target), (2 * source + 1, 2 * target + 1)]
            self.hops[turn] = hops

    def send(self, value, turn):
        with jax.named_scope("ring_send"):
            return Box(lax.ppermute(value, "dp", self.hops[turn]))

    def swap(self, value):
        with jax.named_scope("core_swap"):
            return Box(lax.ppermute(value, "dp", self.core_swap))

    def steps(self, portion):
        total = self.chips // 2
        return range(total * portion // PORTIONS + 1, total * (portion + 1) // PORTIONS + 1)


class Gather:
    def __init__(self, ring, own):
        self.ring = ring
        box = Box(own)
        self.blocks = {(0, 0): [box]}
        self.front = {1: box, -1: box}
        self.fresh = [((0, 0), box)]
        self.pending = [box]

    def swap(self, boxes=None):
        if boxes is None:
            boxes, self.fresh = self.fresh, []
        for (at, _), box in boxes:
            other = self.ring.swap(box.value)
            self.blocks.setdefault((at, 1), []).append(other)
            self.pending.append(other)

    def advance(self, portion):
        chips = self.ring.chips
        came, self.fresh = self.fresh, []
        for step in self.ring.steps(portion):
            for turn in (1, -1):
                value = self.front[turn].value
                if 2 * step == chips:
                    half = value.shape[1] // 2
                    value = value[:, :half] if turn == 1 else value[:, half:]
                box = self.ring.send(value, turn)
                key = (-turn * step % chips, 0)
                self.blocks.setdefault(key, []).append(box)
                self.front[turn] = box
                self.fresh.append((key, box))
                self.pending.append(box)
        self.swap(came)

    def boxes(self):
        waiting, self.pending = self.pending, []
        return waiting

    def ordered(self):
        out = []
        for core in range(2):
            for at in range(self.ring.chips):
                parts = [box.value for box in self.blocks[at, core]]
                out.append(parts[0] if len(parts) == 1 else jnp.concatenate(parts, axis=1))
        return out


class Scatter:
    def __init__(self, ring, grads):
        self.ring = ring
        self.grads = grads
        self.other = Box(grads(1, None))
        self.own = None
        self.got = []
        self.out = []

    def swap(self):
        self.other = self.ring.swap(self.other.value)

    def join(self):
        self.own = Box(self.grads(0, self.other.value))

    def hop(self, portion):
        chips = self.ring.chips
        for step in self.ring.steps(portion):
            self.send()
            away = chips // 2 - step + 1
            kind = {1: "first", 2: "second"}.get(step, "middle")
            got = [box.value for box in self.got]
            out = ring_hop(kind, self.own.value, got, self.ring.around, away, chips - away)
            self.out = [Box(o) for o in out]

    def send(self):
        if self.out:
            self.got = [self.ring.send(self.out[0].value, 1), self.ring.send(self.out[1].value, -1)]
            self.out = []

    def boxes(self):
        return [self.other if self.own is None else self.own] + self.got

    def parts(self):
        return [self.own.value, self.got[0].value, self.got[1].value]


class Exchange:
    def __init__(self, part, pieces):
        self.part = part
        blocks = part.shape[0] // 32
        self.cuts = [32 * (blocks * i // pieces) for i in range(pieces + 1)]
        self.got = []

    def advance(self):
        at = len(self.got)
        self.got.append(Box(swap_tensor(self.part[self.cuts[at] : self.cuts[at + 1]])))
        return self.got[-1]

    def result(self):
        other = jnp.concatenate([box.value for box in self.got], axis=0)
        return self.part.astype(F32) + other.astype(F32)


def swap_tensor(value):
    with jax.named_scope("tensor_swap"):
        return lax.ppermute(value, "tensor", [(0, 1), (1, 0)])


def norm_back(values, scale, gain, grad):
    scaled = gain * grad
    inner = jnp.mean(values * scaled, axis=-1, keepdims=True)
    gain_grad = jnp.sum(values * scale * grad, axis=0)
    return scale * scaled - values * (scale * scale * scale) * inner, gain_grad


def matmul(left, right, dims):
    return lax.dot_general(left, right, dims, preferred_element_type=F32)


def even_blocks(matrix):
    return [matrix[i : i + 128] for i in range(0, matrix.shape[0], 128)]


def unit_chunks(units):
    tile = 256
    cut = units // tile * 3 // 4 * tile
    return [(0, cut), (cut, units)]


def body(
    tokens,
    segments,
    cotangent,
    norm_gain,
    attn_weight,
    beta_weight,
    conv_weight,
    out_gain,
    mlp_gain,
    mlp_weight,
):
    seg_ids = segments[0]
    length = tokens.shape[0]
    devices = lax.axis_size("dp")
    ring = Ring(devices)
    rows, _, local_width = attn_weight.shape
    head_count = beta_weight.shape[1]
    piece = conv_weight.shape[3]
    units = mlp_weight.shape[2]
    width = rows * devices
    groups = head_count // HEADS_PER_STEP
    wide = local_width // groups
    qkv = 3 * local_width
    taps_size = conv_weight.size
    chunks = unit_chunks(units)

    attn_local = pack_mixer(attn_weight, wide)
    small = jnp.concatenate(
        [norm_gain, mlp_gain, beta_weight.reshape(-1), conv_weight.reshape(-1), out_gain]
    ).astype(BF16)
    small = jnp.broadcast_to(small, (devices,) + small.shape)
    mlp_low = mlp_weight.astype(BF16)
    mlp_local = [
        Box(mlp_low[:, :, low:high].reshape(rows, 3 * (high - low))) for low, high in chunks
    ]

    in_ring = rows % 128 == 0
    if in_ring:
        attn = Gather(ring, attn_local)
        attn.advance(0)
    small = Box(lax.all_to_all(small, "dp", 0, 0, tiled=True))
    if in_ring:
        sync(*attn.boxes())
        attn.advance(1)
        sync(*attn.boxes(), small, *mlp_local)
        attn.advance(2)
    at = [0, rows, 2 * rows, 2 * rows + rows * head_count]
    small = small.value
    gain_in = small[:, at[0] : at[1]].reshape(-1).astype(F32)
    gain_mid = small[:, at[1] : at[2]].reshape(-1).astype(F32)
    beta_mat = small[:, at[2] : at[3]].reshape(width, head_count)
    beta_pad = Box(jnp.pad(beta_mat, ((0, 0), (0, 128 - head_count))))
    taps = small[:, at[3] : at[3] + taps_size].reshape(devices, 3, 4, head_count, piece)
    taps = Box(taps.transpose(1, 2, 3, 0, 4).reshape(3, 4, local_width).astype(F32))
    gain_heads = Box(small[:, at[3] + taps_size :].reshape(1, -1).astype(F32))
    inputs_f = tokens.astype(F32)
    scale_in = lax.rsqrt(jnp.mean(inputs_f * inputs_f, axis=-1, keepdims=True) + 1e-05)
    normed = Box((inputs_f * scale_in * gain_in).astype(BF16))
    logits = Box(matmul(normed.value, beta_pad.value, NN))
    if in_ring:
        sync(*attn.boxes(), normed, logits, taps, gain_heads, beta_pad, *mlp_local)
        attn.advance(3)
        sync(*attn.boxes(), normed, mlp_local[1])
        attn.swap()
        attn_blocks = attn.ordered()
        table = ring.table
    else:
        attn_blocks = even_blocks(lax.all_gather(attn_local, "dp", axis=0, tiled=True))
        table = jnp.arange(width // 128, dtype=jnp.int32)
    mats = [lax.all_gather(mlp_local[0].value, "dp", axis=0, tiled=True)]

    half = qkv // 2
    span = groups // 2
    projected = Box(times_rows(normed.value, attn_blocks, table, 0, qkv, 512, F32))
    sync(projected, mlp_local[1])
    mats.append(lax.all_gather(mlp_local[1].value, "dp", axis=0, tiled=True))
    mixed, *saved = mixer_forward(
        projected.value, logits.value, taps.value, gain_heads.value, seg_ids, HEADS_PER_STEP, PASSES, 0
    )
    part = times_turned([([mixed], attn_blocks, qkv)], table)
    hidden = inputs_f + part.astype(F32) + swap_tensor(part).astype(F32)
    scale_mid = lax.rsqrt(jnp.mean(hidden * hidden, axis=-1, keepdims=True) + 1e-05)
    normed_mlp = Box((hidden * scale_mid * gain_mid).astype(BF16))

    acts = []

    def gated(which):
        acts.append(Box(gated_units(normed_mlp.value, cotangent, mats[which], table, 256)))

    def mlp_grads(which):
        def grads(core, plus):
            act = acts[which].value
            size = act.shape[2]
            tile = size // 2 if size % 512 == 0 else size
            pairs = [(normed_mlp.value, act, 0, 2), (cotangent, act, 2, 1)]
            return weight_grads(pairs, tile, rows, ring.cores, core, plus)

        return grads

    def turned(which, kind, plus):
        act = acts[which].value
        return Box(
            units_turned([(act, p, mats[which]) for p in range(2)], 256, kind, table, plus=plus)
        )

    gated(0)
    sums = [Scatter(ring, mlp_grads(0))]
    sync(*sums[0].boxes(), *acts)
    sums[0].swap()
    part = turned(0, F32, None)
    sync(part, *sums[0].boxes(), *acts)
    sums[0].join()
    sums[0].hop(0)
    sync(*sums[0].out, normed_mlp)
    sums[0].send()
    gated(1)
    part = turned(1, BF16, part.value)
    sync(part, *sums[0].boxes())
    exchange = Exchange(part.value, 3)
    piece_a = exchange.advance()
    sums[0].hop(1)
    sync(*sums[0].out, *acts)
    sums[0].send()
    sums.append(Scatter(ring, mlp_grads(1)))
    sync(piece_a, *sums[1].boxes(), *acts)
    sums[1].swap()
    piece_b = exchange.advance()
    down = Box(units_turned([(a.value, 2, mat) for a, mat in zip(acts, mats)], 256, BF16, table))
    sync(piece_b, down, *sums[1].boxes(), *acts)
    piece_c = exchange.advance()
    sums[1].join()
    sync(*sums[0].boxes(), *sums[1].boxes())
    sums[0].hop(2)
    sums[0].send()
    sync(piece_c)

    grad_norm, grad_gain_mid = norm_back(hidden, scale_mid, gain_mid, exchange.result())
    grad_hidden = cotangent.astype(F32) + grad_norm
    grad_hidden_low = Box(grad_hidden.astype(BF16))
    grad_mixed = Box(
        times_rows(grad_hidden_low.value, attn_blocks, table, qkv, local_width, 512, F32)
    )
    sync(grad_mixed, grad_hidden_low, down)
    down = Exchange(down.value, 4)
    back = []

    def mixer_grads():
        group = len(back)
        made = mixer_backward(
            projected.value,
            logits.value,
            taps.value,
            gain_heads.value,
            seg_ids,
            saved,
            grad_mixed.value,
            HEADS_PER_STEP,
            PASSES,
            group,
            group,
        )
        back.append([Box(m) for m in made])

    def early_grads(core, plus):
        pairs = [(normed.value, b[0].value, 0, 1) for b in back[:span]]
        pairs.append((grad_hidden_low.value, mixed, 0, 1))
        return weight_grads(pairs, 256, rows, ring.cores, core, plus)

    def late_grads(core, plus):
        pairs = [(normed.value, b[0].value, 0, 1) for b in back[span:]]
        return weight_grads(pairs, 3 * wide, rows, ring.cores, core, plus)

    quarter = [groups * i // 4 for i in range(5)]

    def mixer_grads_to(count):
        while len(back) < count:
            mixer_grads()

    mixer_grads_to(quarter[1])
    sync(down.advance(), *sums[0].boxes(), back[-1][0], grad_mixed)
    sums[0].hop(3)
    sync(*sums[0].out, grad_mixed)
    sums[0].send()
    mixer_grads_to(quarter[2])
    first = Scatter(ring, early_grads)
    sync(down.advance(), *first.boxes(), *sums[0].boxes(), *sums[1].boxes(), grad_mixed)
    first.swap()
    sums[1].hop(0)
    sync(*sums[1].out, grad_mixed)
    sums[1].send()
    mixer_grads_to(quarter[3])
    sync(down.advance(), *first.boxes(), *sums[1].boxes(), back[-1][0], grad_mixed)
    sums[1].hop(1)
    sync(*sums[1].out, *first.boxes())
    sums[1].send()
    first.join()
    sync(down.advance(), *first.boxes(), *sums[1].boxes(), grad_mixed)
    sums[1].hop(2)
    first.hop(0)
    sync(*sums[1].out, *first.out, grad_mixed)
    sums[1].send()
    first.send()
    mixer_grads_to(groups)
    sync(*first.boxes(), *sums[1].boxes(), *[b[0] for b in back])
    sums[1].hop(3)
    first.hop(1)
    sync(*sums[1].out, *first.out, *[b[0] for b in back])
    sums[1].send()
    first.send()
    second = Scatter(ring, late_grads)
    grad_logits_low = Box(sum(b[1].value for b in back).astype(BF16))
    sync(*second.boxes(), *[b[0] for b in back], grad_logits_low)
    part = Box(
        times_turned(
            [([b[0].value for b in back], attn_blocks, 0)],
            table,
            extra=(grad_logits_low.value, beta_pad.value),
        )
    )
    sync(part, *first.boxes(), *sums[1].boxes(), *[b[0] for b in back], *second.boxes(), grad_logits_low)
    exchange = Exchange(part.value, 3)
    piece_a = exchange.advance()
    second.swap()
    first.hop(2)
    sync(*first.out, *sums[1].boxes(), grad_logits_low)
    first.send()
    mlp_grad = Box(units_result([s.parts() for s in sums], ring.around))
    grad_beta = Box(matmul(normed.value, grad_logits_low.value, TN)[:, :head_count])
    sync(piece_a, mlp_grad, grad_beta, *first.boxes(), *second.boxes(), *[b[0] for b in back])
    piece_b = exchange.advance()
    second.join()
    second.hop(0)
    first.hop(3)
    sync(*second.out, *first.out, grad_beta)
    second.send()
    first.send()
    grad_gain_heads = sum(b[3].value[0] for b in back)
    grad_gain_heads = grad_gain_heads + swap_tensor(grad_gain_heads)
    grad_taps = jnp.concatenate([b[2].value for b in back], axis=2)
    grad_taps = grad_taps.reshape(3, 4, head_count, devices, piece).transpose(3, 0, 1, 2, 4)
    early = [grad_gain_mid, grad_beta.value, grad_taps, grad_gain_heads]
    early = Box(jnp.concatenate([value.reshape(devices, -1) for value in early], axis=1))
    sync(piece_b, early, *second.boxes(), *first.boxes())
    piece_c = exchange.advance()
    second.hop(1)
    sync(early, *second.out)
    second.send()
    early = Box(lax.all_to_all(early.value, "dp", 0, 0, tiled=True))
    result = Box((hidden + down.result()).astype(BF16))
    sync(piece_c, result, *second.boxes())
    second.hop(2)
    second.send()
    sync(early, *second.boxes())
    second.hop(3)
    second.send()

    grad_first, grad_gain_in = norm_back(inputs_f, scale_in, gain_in, exchange.result())
    grad_inputs = grad_hidden + grad_first

    late = lax.all_to_all(grad_gain_in.reshape(devices, -1), "dp", 0, 0, tiled=True)
    packed = jnp.concatenate([jnp.sum(late, axis=0), jnp.sum(early.value, axis=0)])
    attn_grad = mixer_result([first.parts(), second.parts()], wide, local_width, ring.around)
    return (
        result.value,
        grad_inputs,
        packed[at[0] : at[1]],
        attn_grad,
        packed[at[2] : at[3]].reshape(rows, head_count),
        packed[at[3] : at[3] + taps_size].reshape(conv_weight.shape),
        packed[at[3] + taps_size :],
        packed[at[1] : at[2]],
        mlp_grad.value.transpose(1, 0, 2),
    )


def solution(mesh):
    return jax.shard_map(
        body,
        mesh=mesh,
        in_specs=(
            P("dp", None),
            P("dp", None),
            P("dp", None),
            P("dp"),
            P("dp", None, "tensor"),
            P("dp", "tensor"),
            P(None, None, "tensor", "dp"),
            P("dp"),
            P("dp"),
            P("dp", None, "tensor"),
        ),
        out_specs=(
            P("dp", None),
            P("dp", None),
            P("dp"),
            P("dp", None, "tensor"),
            P("dp", "tensor"),
            P(None, None, "tensor", "dp"),
            P("dp"),
            P("dp"),
            P("dp", None, "tensor"),
        ),
        check_vma=False,
    )
```
